32 devices in a mesh: group: 8 (over z, core), tensor: 4 (over y, x).
Axes of the slice: x: 2, y: 2, z: 4, core: 2. Of those that a mesh axis runs over, the one named last changes fastest.
Arguments:
- queries: bfloat16 [96, 4, 8192], P('group', None, 'tensor'), may hold values from -603 to 603
- new_entries: bfloat16 [96, 4, 2048], P('group'), may hold values from -6 to 6
- resident_cache: bfloat16 [32, 512, 2048], P('group', 'tensor'), may hold values from -6 to 6
- prefill_cache: bfloat16 [64, 512, 2048], P('group', 'tensor'), may hold values from -6 to 6
- resident_kept: int32 [32], replicated, may hold values from 256 to 512, as said below
- kept_tokens: int32 [64], replicated, may hold values from 1 to 512, as said below
- prefill_slot: int32 [64], replicated, may hold values from 0 to 63, as said below
- decode_slot: int32 [64], replicated, may hold values from 4 to 95, as said below
Outputs:
- attended: bfloat16 [96, 4, 8192], P('group', None, 'tensor')
The draws below stay inside these ranges and needn't reach their ends.
Inputs may be any that keep to these rules, and one draw needn't show every extreme that they name: `kept_tokens`: some request keeps exactly 512 positions. `prefill_slot`: A permutation of the 64 prefill slots; slot s lies in prefill group s // 8. `decode_slot`: every slot g * 12 + l with l >= 4 is named by exactly one request; from one prefill group to one decode group go at most 1 request, and exactly 1 for some pairs. `resident_kept`: some resident request keeps exactly 512 positions.
All inputs are finite; a program needn't handle non-finite values.
Results may differ from the reference program's by a relative error of at most 0.0044.
Values may be sent and summed in bfloat16 or wider, within the bound.
A program may use at most 128 MiB of HBM per device.

```python
import math
import jax
import jax.numpy as jnp
from jax import lax

H = 64
KVH = 8
HD = 128
STEPS = 4
CAP = 512
MIG_DEV = 8
RES_DEV = 4
DSLOTS = 96
REQS = 64
PAIR_MOST = 1
N_GROUP = 8


def migration_plan(key):
    base = jax.random.fold_in(key, 7)
    subkeys = jax.random.split(base, 5)
    slot_count = MIG_DEV * N_GROUP
    rotation = jax.random.randint(subkeys[0], (), 0, 4)
    every_slot = jnp.arange(slot_count, dtype=jnp.int32)
    home_group = every_slot // MIG_DEV
    home_local = every_slot % MIG_DEV
    load_level = 1 + (home_group + rotation) % 4
    jitter = jax.random.randint(subkeys[1], (slot_count,), 0, CAP // 8)
    jitter = jnp.where((load_level == 4) & (home_local == 0), 0, jitter)
    kept_by_slot = load_level * (CAP // 4) - jitter
    group_order = jax.random.permutation(subkeys[2], N_GROUP).astype(jnp.int32)
    local_order = jax.random.permutation(subkeys[3], MIG_DEV).astype(jnp.int32)
    lane_index = home_local // PAIR_MOST
    target_group = group_order[(home_group + lane_index) % N_GROUP]
    target_local = RES_DEV + local_order[lane_index * PAIR_MOST + home_local % PAIR_MOST]
    target_slot = target_group * (RES_DEV + MIG_DEV) + target_local
    request_slot = jax.random.permutation(subkeys[4], slot_count).astype(jnp.int32)
    return (kept_by_slot[request_slot], request_slot, target_slot[request_slot])


def draw_kept_tokens(key, part):
    return migration_plan(key)[0].astype(jnp.int32)


def draw_prefill_slot(key, part):
    return migration_plan(key)[1].astype(jnp.int32)


def draw_decode_slot(key, part):
    return migration_plan(key)[2].astype(jnp.int32)


def draw_resident_kept(key, part):
    sub_key = jax.random.fold_in(key, 11)
    picked = jax.random.randint(sub_key, (N_GROUP * RES_DEV,), CAP // 2, CAP + 1)
    return jnp.where(jnp.arange(N_GROUP * RES_DEV) == 0, CAP, picked).astype(jnp.int32)


def token_draws(key):
    base = jax.random.fold_in(key, 23)
    subkeys = jax.random.split(base, 2)
    row_total = DSLOTS
    new_part = jnp.clip(jax.random.normal(subkeys[0], (row_total, STEPS, 2, KVH, HD), jnp.float32), -6.0, 6.0)
    spread_part = jnp.clip(jax.random.normal(subkeys[1], (row_total, STEPS, KVH, H // KVH, HD), jnp.float32), -6.0, 6.0)
    asking = spread_part + 0.5 * new_part[:, :, 0, :, None, :]
    return (asking.reshape(row_total, STEPS, H * HD), new_part.reshape(row_total, STEPS, 2 * KVH * HD))


def draw_queries(key, part):
    return token_draws(key)[0].astype(jnp.bfloat16)


def draw_new_entries(key, part):
    return token_draws(key)[1].astype(jnp.bfloat16)


def level_of(own_key, dims, cuts, smallest, largest):
    level = 1.0
    for position, parts in cuts:
        heights = jax.random.uniform(jax.random.fold_in(jax.random.fold_in(own_key, 6), position), (parts,), jnp.float32, smallest / len(cuts), largest / len(cuts))
        level = level * jnp.repeat(jnp.exp(heights), dims[position] // parts).reshape((-1,) + (1,) * (len(dims) - 1 - position))
    return level


def centred(own_key, shape, spread, reach, shards=(), kind=jnp.bfloat16):
    factor_of = level_of(own_key, shape, shards, -0.22, 0.18) if shards else 1.0
    result = jax.random.normal(own_key, shape, jnp.float32) * spread * factor_of
    return jnp.minimum(jnp.maximum(result, -reach), reach).astype(kind)


def setup_inputs(seed: int = 0) -> dict:
    splits = jax.random.split(jax.random.key(seed), 9)
    return {
        "queries": draw_queries(jax.random.fold_in(splits[8], 71), 0),
        "new_entries": draw_new_entries(jax.random.fold_in(splits[8], 71), 0),
        "resident_cache": centred(splits[2], (N_GROUP * RES_DEV, CAP, 2 * KVH * HD), 1.0, 6.0, ((0, 8), (1, 4))),
        "prefill_cache": centred(splits[3], (REQS, CAP, 2 * KVH * HD), 1.0, 6.0, ((0, 8), (1, 4))),
        "resident_kept": draw_resident_kept(jax.random.fold_in(splits[8], 71), 0),
        "kept_tokens": draw_kept_tokens(jax.random.fold_in(splits[8], 71), 0),
        "prefill_slot": draw_prefill_slot(jax.random.fold_in(splits[8], 71), 0),
        "decode_slot": draw_decode_slot(jax.random.fold_in(splits[8], 71), 0),
    }


def attend_one(asking, newest_in, stored, length):
    sharing = H // KVH
    temper = 1.0 / math.sqrt(HD)
    asked_rows = asking.astype(jnp.float32).reshape(STEPS, KVH, sharing, HD)
    entries = stored.astype(jnp.float32).reshape(CAP, 2, KVH, HD)
    newest = newest_in.astype(jnp.float32).reshape(STEPS, 2, KVH, HD)
    old_scores = jnp.einsum('tkgd,pkd->tkgp', asked_rows, entries[:, 0]) * temper
    new_scores = jnp.einsum('tkgd,ukd->tkgu', asked_rows, newest[:, 0]) * temper
    old_usable = (jnp.arange(CAP) < length)[None, None, None, :]
    new_usable = (jnp.arange(STEPS)[None, :] <= jnp.arange(STEPS)[:, None])[:, None, None, :]
    highest = jnp.maximum(lax.optimization_barrier(jnp.max(jnp.where(old_usable, old_scores, -1e+30), axis=3)), lax.optimization_barrier(jnp.max(jnp.where(new_usable, new_scores, -1e+30), axis=3)))
    old_weights = jnp.where(old_usable, jnp.exp(old_scores - highest[..., None]), 0.0)
    new_weights = jnp.where(new_usable, jnp.exp(new_scores - highest[..., None]), 0.0)
    totals = lax.optimization_barrier(jnp.sum(old_weights, axis=3)) + lax.optimization_barrier(jnp.sum(new_weights, axis=3))
    old_rounded = lax.optimization_barrier(old_weights.astype(jnp.bfloat16)).astype(jnp.float32)
    new_rounded = lax.optimization_barrier(new_weights.astype(jnp.bfloat16)).astype(jnp.float32)
    blended = jnp.einsum('tkgp,pkd->tkgd', old_rounded, entries[:, 1]) + jnp.einsum('tkgu,ukd->tkgd', new_rounded, newest[:, 1])
    return (blended / totals[..., None]).reshape(STEPS, H * HD).astype(jnp.bfloat16)

def reference(queries, new_entries, resident_cache, prefill_cache, resident_kept, kept_tokens, prefill_slot, decode_slot):
    per_group = RES_DEV + MIG_DEV
    total_slots = N_GROUP * per_group
    source = jnp.zeros((total_slots,), jnp.int32).at[decode_slot].set(prefill_slot.astype(jnp.int32))
    moved_len = jnp.zeros((total_slots,), jnp.int32).at[decode_slot].set(kept_tokens.astype(jnp.int32))
    everyone = jnp.arange(total_slots, dtype=jnp.int32)
    owner_group = everyone // per_group
    within = everyone % per_group
    is_resident = within < RES_DEV
    resident_row = (owner_group * RES_DEV + jnp.minimum(within, RES_DEV - 1)).astype(jnp.int32)
    lengths = jnp.where(is_resident, resident_kept[resident_row], moved_len)

    def handle(record):
        slot_id, resident_id, source_id, is_local, length = record
        stored = jnp.where(is_local, resident_cache[resident_id], prefill_cache[source_id])
        return attend_one(queries[slot_id], new_entries[slot_id], stored, length)
    return lax.map(handle, (everyone, resident_row, source, is_resident, lengths))
```

```python
import functools
import math

import jax
import jax.numpy as jnp
from jax import lax
from jax.experimental import pallas as pl
from jax.experimental.pallas import tpu as pltpu
from jax.sharding import PartitionSpec as P

H = 64
KVH = 8
HD = 128
STEPS = 4
MIG_DEV = 8
RES_DEV = 4
PER_GROUP = RES_DEV + MIG_DEV
BATCH = 4

NEG_FLOOR = -1e30
SCALE = 1.0 / math.sqrt(HD)
MESH = pl.DeviceIdType.MESH
F32 = jnp.float32
BF16 = jnp.bfloat16
NT = (((1,), (1,)), ((), ()))
TN = (((0,), (0,)), ((), ()))


def kernel(
    G,
    T,
    tbl,
    kept,
    q_in,
    new_in,
    res_hbm,
    pre_hbm,
    out,
    res,
    pre,
    qall,
    zq,
    stage,
    obuf,
    rbuf,
    sbuf,
    rstat,
    statbuf,
    facbuf,
    zo,
    zro,
    zs,
    zrs,
    newk,
    fin,
    cache_sem,
    zq_s,
    zq_r,
    rq_s,
    rq_r,
    f_s,
    f_r,
    o_s,
    o_r,
    st_s,
    st_r,
    zo_s,
    zo_r,
    zs_s,
    zs_r,
):
    KVL = max(1, KVH // T)
    HB = H // T
    HU = HB // KVL
    R = STEPS * HU
    LW = BATCH * R
    SW = 2 * KVL
    NB = 1 + G // BATCH
    pos = res.shape[1]
    half = KVH * HD
    g = lax.axis_index("group")
    t = lax.axis_index("tensor")
    offset = t * pos

    def peer_t(k):
        return lax.rem(t + k, T)

    def peer_g(k):
        return lax.rem(g + k, G)

    def from_g(k):
        return lax.rem(g - k + G, G)

    def over_t(src, dst, ssem, rsem, dev):
        return pltpu.make_async_remote_copy(
            src_ref=src, dst_ref=dst, send_sem=ssem, recv_sem=rsem,
            device_id=(g, dev), device_id_type=MESH,
        )

    def over_g(src, dst, ssem, rsem, dev):
        return pltpu.make_async_remote_copy(
            src_ref=src, dst_ref=dst, send_sem=ssem, recv_sem=rsem,
            device_id=(dev, t), device_id_type=MESH,
        )

    def c_zq(k):
        return over_g(zq.at[k], qall.at[t, RES_DEV + k], zq_s.at[k], zq_r.at[k], peer_g(k))

    def c_rq(k):
        p = peer_t(k)
        own = qall.at[t, pl.ds(0, RES_DEV)]
        return over_t(own, own, rq_s.at[k], rq_r.at[k], p)

    def c_fwd(k, n):
        own = qall.at[t, RES_DEV + k]
        return over_t(own, own, f_s.at[k, n], f_r.at[k, n], peer_t(n))

    def c_o(b, n):
        p = peer_t(n)
        return over_t(obuf.at[b, p], rbuf.at[b, n], o_s.at[b, n], o_r.at[b, n], p)

    def c_st(b, n):
        p = peer_t(n)
        return over_t(sbuf.at[b, p], rstat.at[b, n], st_s.at[b, n], st_r.at[b, n], p)

    def c_zo(k):
        return over_g(zo.at[k], zro.at[k], zo_s.at[k], zo_r.at[k], from_g(k))

    def c_zs(k):
        return over_g(zs.at[k // BATCH], zrs.at[k], zs_s.at[k], zs_r.at[k], from_g(k))

    load_res = pltpu.make_async_copy(res_hbm, res, cache_sem.at[0])
    load_pre = pltpu.make_async_copy(pre_hbm, pre, cache_sem.at[1])
    load_res.start()
    load_pre.start()

    barrier = pltpu.get_barrier_semaphore()
    for k in range(1, G):
        pl.semaphore_signal(barrier, inc=1, device_id=(peer_g(k), t), device_id_type=MESH)
    for k in range(1, T):
        pl.semaphore_signal(barrier, inc=1, device_id=(g, peer_t(k)), device_id_type=MESH)

    def arranged(row, slot):
        for h in range(HB):
            piece = q_in[row, :, h * HD : (h + 1) * HD]
            stage[slot, h * STEPS : (h + 1) * STEPS, :] = piece.astype(F32)
        return stage[slot].astype(BF16)

    for k in range(G):
        block = arranged(tbl[0, peer_g(k)], k)
        zq[k] = block
        if k == 0:
            qall[t, RES_DEV] = block
    for j in range(RES_DEV):
        qall[t, j] = arranged(j, G + j)

    pl.semaphore_wait(barrier, G - 1 + T - 1)
    for k in range(1, G):
        c_zq(k).start()
    for n in range(1, T):
        c_rq(n).start()
    for n in range(1, T):
        c_fwd(0, n).start()

    kv_col = pl.multiple_of((t * KVL * KVH) // (T * KVL) * HD, HD)
    for b in range(NB):
        for j in range(BATCH):
            row = j if b == 0 else tbl[0, peer_g((b - 1) * BATCH + j)]
            lo = j * STEPS
            newk[b, 0, lo : lo + STEPS, :] = new_in[row, :, pl.ds(kv_col, KVL * HD)].astype(F32)
            newk[b, 1, lo : lo + STEPS, :] = new_in[
                row, :, pl.ds(pl.multiple_of(half + kv_col, HD), KVL * HD)
            ].astype(F32)

    for k in range(1, G):
        c_zq(k).wait_recv()
        for n in range(1, T):
            c_fwd(k, n).start()

    def attend_slot(cache, row, length, slot, b, j):
        lane = lax.broadcasted_iota(jnp.int32, (R, 128), 1)
        usable = offset + lax.broadcasted_iota(jnp.int32, (R, pos), 1) < length
        stat = jnp.zeros((R, 128), F32)
        rows = pl.ds(pl.multiple_of(j * R, R), R)
        for tt in range(T):
            for i in range(KVL):
                kv = (tt * KVL + i) * KVH // (T * KVL)
                asked = qall[tt, slot, i * R : (i + 1) * R, :]
                keys = cache[row, :, kv * HD : (kv + 1) * HD]
                values = cache[row, :, half + kv * HD : half + (kv + 1) * HD]
                scores = lax.dot_general(asked, keys, NT, preferred_element_type=F32) * SCALE
                scores = jnp.where(usable, scores, NEG_FLOOR)
                highest = jnp.max(scores, axis=1, keepdims=True)
                weights = jnp.where(usable, jnp.exp(scores - highest), 0.0)
                total = jnp.sum(weights, axis=1, keepdims=True)
                blended = jnp.dot(weights.astype(BF16), values, preferred_element_type=F32)
                obuf[b, tt, i, rows, :] = blended.astype(BF16)
                stat = jnp.where(lane == tt * SW + i, highest, stat)
                stat = jnp.where(lane == tt * SW + KVL + i, total, stat)
        statbuf[rows, :] = stat

    def send_batch(b):
        turned = statbuf[...].T
        for tt in range(T):
            sbuf[b, tt] = turned[tt * SW : tt * SW + 8, :]
        for n in range(1, T):
            c_st(b, n).start()
            c_o(b, n).start()
        rbuf[b, 0] = obuf[b, t]
        rstat[b, 0] = sbuf[b, t]

    load_res.wait()
    for n in range(1, T):
        c_rq(n).wait_recv()

    @pl.loop(0, RES_DEV)
    def _(j):
        attend_slot(res, j, kept[g * RES_DEV + j], j, 0, j)

    send_batch(0)
    load_pre.wait()

    @pl.loop(1, NB)
    def _(b):
        @pl.loop(0, BATCH)
        def _(j):
            k = (b - 1) * BATCH + j
            for n in range(1, T):
                c_fwd(k, n).wait_recv()
            source = from_g(k)
            attend_slot(pre, tbl[1, source], tbl[2, source], RES_DEV + k, b, j)

        send_batch(b)

    def merged(b):
        for n in range(1, T):
            c_st(b, n).wait_recv()
            c_o(b, n).wait_recv()
        tops = [rstat[b, n][:KVL] for n in range(T)]
        highest = functools.reduce(jnp.maximum, tops)
        total = jnp.zeros((KVL, LW), F32)
        for n in range(T):
            factor = jnp.exp(tops[n] - highest)
            total = total + factor * rstat[b, n][KVL:SW]
            facbuf[n * KVL : (n + 1) * KVL, :] = factor
        columns = facbuf[...].T
        blended = []
        for i in range(KVL):
            sum_i = jnp.zeros((LW, HD), F32)
            for n in range(T):
                c = n * KVL + i
                sum_i = sum_i + rbuf[b, n, i].astype(F32) * columns[:, c : c + 1]
            blended.append(sum_i)
        return highest, total, blended

    def finish(b, highest, total, blended, asked):
        r16 = lax.broadcasted_iota(jnp.int32, (BATCH * STEPS, LW), 0)
        lanes = lax.broadcasted_iota(jnp.int32, (BATCH * STEPS, LW), 1)
        causal = (r16 // STEPS == lanes // R) & (r16 % STEPS <= lanes % STEPS)
        adds = []
        for i in range(KVL):
            keys = newk[b, 0, :, i * HD : (i + 1) * HD].astype(BF16)
            values = newk[b, 1, :, i * HD : (i + 1) * HD].astype(BF16)
            scores = lax.dot_general(keys, asked[i], NT, preferred_element_type=F32) * SCALE
            scores = jnp.where(causal, scores, NEG_FLOOR)
            top = jnp.maximum(highest[i : i + 1], jnp.max(scores, axis=0, keepdims=True))
            weights = jnp.where(causal, jnp.exp(scores - top), 0.0)
            carried = jnp.exp(highest[i : i + 1] - top)
            inverse = 1.0 / (total[i : i + 1] * carried + jnp.sum(weights, axis=0, keepdims=True))
            facbuf[i : i + 1, :] = carried
            facbuf[KVL + i : KVL + i + 1, :] = inverse
            adds.append(
                lax.dot_general(weights.astype(BF16), values, TN, preferred_element_type=F32)
            )
        columns = facbuf[...].T
        for i in range(KVL):
            done = blended[i] * columns[:, i : i + 1] + adds[i]
            done = done * columns[:, KVL + i : KVL + i + 1]
            for j in range(BATCH):
                fin[b * BATCH + j, i * R : (i + 1) * R, :] = done[j * R : (j + 1) * R]

    def put(slot, row):
        for h in range(HB):
            piece = fin[slot, h * STEPS : (h + 1) * STEPS, :]
            out[row, :, h * HD : (h + 1) * HD] = piece.astype(BF16)

    for b in range(1, NB):
        highest, total, blended = merged(b)
        packed = jnp.concatenate([highest, total], axis=0)
        zs[b - 1, 0:SW, :] = packed
        for j in range(BATCH):
            k = (b - 1) * BATCH + j
            for i in range(KVL):
                zo[k, i] = blended[i][j * R : (j + 1) * R].astype(BF16)
            if k:
                c_zs(k).start()
                c_zo(k).start()
            else:
                zrs[0] = zs[0]
                zro[0] = zo[0]

    def queries_of(b):
        return [
            jnp.concatenate(
                [
                    (qall[t, j] if b == 0 else zq[(b - 1) * BATCH + j])[i * R : (i + 1) * R]
                    for j in range(BATCH)
                ],
                axis=0,
            )
            for i in range(KVL)
        ]

    finish(0, *merged(0), queries_of(0))
    for j in range(RES_DEV):
        put(j, j)

    for b in range(1, NB):
        lanes = lax.broadcasted_iota(jnp.int32, (8, LW), 1)
        stats = jnp.zeros((8, LW), F32)
        for j in range(BATCH):
            k = (b - 1) * BATCH + j
            if k:
                c_zs(k).wait_recv()
                c_zo(k).wait_recv()
            stats = jnp.where(lanes // R == j, zrs[k], stats)
        blended = [
            jnp.concatenate(
                [zro[(b - 1) * BATCH + j, i].astype(F32) for j in range(BATCH)], axis=0
            )
            for i in range(KVL)
        ]
        finish(b, stats[:KVL], stats[KVL:SW], blended, queries_of(b))
    for l in range(MIG_DEV):
        put(RES_DEV + tbl[3, l], RES_DEV + l)

    for k in range(1, G):
        c_zq(k).wait_send()
        c_zs(k).wait_send()
        c_zo(k).wait_send()
    for n in range(1, T):
        c_rq(n).wait_send()

        @pl.loop(0, G)
        def _(k):
            c_fwd(k, n).wait_send()

        @pl.loop(0, NB)
        def _(b):
            c_st(b, n).wait_send()
            c_o(b, n).wait_send()


def routes(kept_tokens, prefill_slot, decode_slot, G):
    g = lax.axis_index("group")
    dest_group, dest_row = decode_slot // PER_GROUP, decode_slot % PER_GROUP
    home_group, home_row = prefill_slot // MIG_DEV, prefill_slot % MIG_DEV
    arriving, leaving = dest_group == g, home_group == g
    width = max(G, MIG_DEV)
    every = jnp.arange(width, dtype=jnp.int32)[:, None]

    def pick(key, wanted, value):
        hit = (key[None] == every) & wanted[None]
        return jnp.sum(jnp.where(hit, value[None], 0), axis=1)

    return jnp.stack(
        [
            pick(home_group, arriving, dest_row),
            pick(dest_group, leaving, home_row),
            pick(dest_group, leaving, kept_tokens),
            pick(dest_row - RES_DEV, arriving, (home_group - g + G) % G),
        ]
    )


def body(
    queries,
    new_entries,
    resident_cache,
    prefill_cache,
    resident_kept,
    kept_tokens,
    prefill_slot,
    decode_slot,
):
    G = lax.axis_size("group")
    T = lax.axis_size("tensor")
    KVL = max(1, KVH // T)
    HB = H // T
    RB = STEPS * HB
    R = RB // KVL
    LW = BATCH * R
    NB = 1 + G // BATCH
    tbl = routes(kept_tokens, prefill_slot, decode_slot, G)
    dma = pltpu.SemaphoreType.DMA
    vmem = pl.BlockSpec(memory_space=pltpu.VMEM)
    smem = pl.BlockSpec(memory_space=pltpu.SMEM)
    hbm = pl.BlockSpec(memory_space=pl.ANY)
    return pl.pallas_call(
        functools.partial(kernel, G, T),
        out_shape=jax.ShapeDtypeStruct(queries.shape, BF16),
        in_specs=[smem, smem, vmem, vmem, hbm, hbm],
        out_specs=vmem,
        scratch_shapes=[
            pltpu.VMEM(resident_cache.shape, BF16),
            pltpu.VMEM(prefill_cache.shape, BF16),
            pltpu.VMEM((T, RES_DEV + G, RB, HD), BF16),
            pltpu.VMEM((G, RB, HD), BF16),
            pltpu.VMEM((G + RES_DEV, RB, HD), F32),
            pltpu.VMEM((NB, T, KVL, LW, HD), BF16),
            pltpu.VMEM((NB, T, KVL, LW, HD), BF16),
            pltpu.VMEM((NB, T, 8, LW), F32),
            pltpu.VMEM((NB, T, 8, LW), F32),
            pltpu.VMEM((LW, 128), F32),
            pltpu.VMEM((128, LW), F32),
            pltpu.VMEM((G, KVL, R, HD), BF16),
            pltpu.VMEM((G, KVL, R, HD), BF16),
            pltpu.VMEM((NB - 1, 8, LW), F32),
            pltpu.VMEM((G, 8, LW), F32),
            pltpu.VMEM((NB, 2, BATCH * STEPS, KVL * HD), F32),
            pltpu.VMEM((NB * BATCH, RB, HD), F32),
            dma((2,)),
            dma((G,)),
            dma((G,)),
            dma((T,)),
            dma((T,)),
            dma((G, T)),
            dma((G, T)),
            dma((NB, T)),
            dma((NB, T)),
            dma((NB, T)),
            dma((NB, T)),
            dma((G,)),
            dma((G,)),
            dma((G,)),
            dma((G,)),
        ],
        compiler_params=pltpu.CompilerParams(collective_id=0, has_side_effects=True),
    )(tbl, resident_kept, queries, new_entries, resident_cache, prefill_cache)


def solution(mesh):
    in_specs = (
        P("group", None, "tensor"),
        P("group", None, None),
        P("group", "tensor", None),
        P("group", "tensor", None),
        P(),
        P(),
        P(),
        P(),
    )
    out_specs = P("group", None, "tensor")
    return jax.shard_map(body, mesh=mesh, in_specs=in_specs, out_specs=out_specs, check_vma=False)
```

```python
import functools
import math

import jax
import jax.numpy as jnp
from jax import lax
from jax.experimental import pallas as pl
from jax.experimental.pallas import tpu as pltpu
from jax.sharding import PartitionSpec as P

H = 64
KVH = 8
HD = 128
STEPS = 4
MIG_DEV = 8
RES_DEV = 4
PER_GROUP = RES_DEV + MIG_DEV
BATCH = 4

NEG_FLOOR = -1e30
SCALE = 1.0 / math.sqrt(HD)
MESH = pl.DeviceIdType.MESH
F32 = jnp.float32
BF16 = jnp.bfloat16
NT = (((1,), (1,)), ((), ()))
TN = (((0,), (0,)), ((), ()))


def kernel(
    G,
    T,
    tbl,
    kept,
    q_in,
    new_in,
    res_hbm,
    pre_hbm,
    out,
    res,
    pre,
    qall,
    zq,
    stage,
    obuf,
    rbuf,
    sbuf,
    rstat,
    statbuf,
    facbuf,
    zo,
    zro,
    zs,
    zrs,
    newk,
    fin,
    cache_sem,
    zq_s,
    zq_r,
    rq_s,
    rq_r,
    f_s,
    f_r,
    o_s,
    o_r,
    st_s,
    st_r,
    zo_s,
    zo_r,
    zs_s,
    zs_r,
):
    KVL = max(1, KVH // T)
    HB = H // T
    HU = HB // KVL
    R = STEPS * HU
    LW = BATCH * R
    SW = 2 * KVL
    NB = 1 + G // BATCH
    pos = res.shape[1]
    half = KVH * HD
    g = lax.axis_index("group")
    t = lax.axis_index("tensor")
    offset = t * pos

    def peer_t(k):
        return lax.rem(t + k, T)

    def peer_g(k):
        return lax.rem(g + k, G)

    def from_g(k):
        return lax.rem(g - k + G, G)

    def over_t(src, dst, ssem, rsem, dev):
        return pltpu.make_async_remote_copy(
            src_ref=src, dst_ref=dst, send_sem=ssem, recv_sem=rsem,
            device_id=(g, dev), device_id_type=MESH,
        )

    def over_g(src, dst, ssem, rsem, dev):
        return pltpu.make_async_remote_copy(
            src_ref=src, dst_ref=dst, send_sem=ssem, recv_sem=rsem,
            device_id=(dev, t), device_id_type=MESH,
        )

    def c_zq(k):
        return over_g(zq.at[k], qall.at[t, RES_DEV + k], zq_s.at[0], zq_r.at[k], peer_g(k))

    def c_rq(k):
        p = peer_t(k)
        own = qall.at[t, pl.ds(0, RES_DEV)]
        return over_t(own, own, rq_s.at[0], rq_r.at[0], p)

    def c_fwd(k, n):
        own = qall.at[t, RES_DEV + k]
        return over_t(own, own, f_s.at[n], f_r.at[k], peer_t(n))

    def c_o(b, n):
        p = peer_t(n)
        return over_t(obuf.at[b, p], rbuf.at[b, n], o_s.at[b], o_r.at[b], p)

    def c_st(b, n):
        p = peer_t(n)
        return over_t(sbuf.at[b, p], rstat.at[b, n], st_s.at[b], st_r.at[b], p)

    def c_zo(k):
        return over_g(zo.at[k], zro.at[k], zo_s.at[0], zo_r.at[k // BATCH], from_g(k))

    def c_zs(k):
        return over_g(zs.at[k // BATCH], zrs.at[k], zs_s.at[0], zs_r.at[k // BATCH], from_g(k))

    load_res = pltpu.make_async_copy(res_hbm, res, cache_sem.at[0])
    load_pre = pltpu.make_async_copy(pre_hbm, pre, cache_sem.at[1])
    load_res.start()
    load_pre.start()

    barrier = pltpu.get_barrier_semaphore()
    for k in range(1, G):
        pl.semaphore_signal(barrier, inc=1, device_id=(peer_g(k), t), device_id_type=MESH)
    for k in range(1, T):
        pl.semaphore_signal(barrier, inc=1, device_id=(g, peer_t(k)), device_id_type=MESH)

    def arranged(row, slot):
        for h in range(HB):
            piece = q_in[row, :, h * HD : (h + 1) * HD]
            stage[slot, h * STEPS : (h + 1) * STEPS, :] = piece.astype(F32)
        return stage[slot].astype(BF16)

    for k in range(G):
        block = arranged(tbl[peer_g(k)], k)
        zq[k] = block
        if k == 0:
            qall[t, RES_DEV] = block
    for j in range(RES_DEV):
        qall[t, j] = arranged(j, G + j)

    pl.semaphore_wait(barrier, G - 1 + T - 1)
    for k in range(1, G):
        c_zq(k).start()
    for n in range(1, T):
        c_rq(n).start()
    for n in range(1, T):
        c_fwd(0, n).start()

    kv_col = pl.multiple_of((t * KVL * KVH) // (T * KVL) * HD, HD)
    for b in range(NB):
        for j in range(BATCH):
            row = j if b == 0 else tbl[peer_g((b - 1) * BATCH + j)]
            lo = j * STEPS
            newk[b, 0, lo : lo + STEPS, :] = new_in[row, :, pl.ds(kv_col, KVL * HD)].astype(F32)
            newk[b, 1, lo : lo + STEPS, :] = new_in[
                row, :, pl.ds(pl.multiple_of(half + kv_col, HD), KVL * HD)
            ].astype(F32)

    for k in range(1, G):
        c_zq(k).wait_recv()
        for n in range(1, T):
            c_fwd(k, n).start()

    def attend_slot(cache, row, length, slot, b, j):
        lane = lax.broadcasted_iota(jnp.int32, (R, 128), 1)
        usable = offset + lax.broadcasted_iota(jnp.int32, (R, pos), 1) < length
        stat = jnp.zeros((R, 128), F32)
        rows = pl.ds(pl.multiple_of(j * R, R), R)
        W = 2 if KVL % 2 == 0 else 1
        units = [(tt, i) for tt in range(T) for i in range(0, KVL, W)]
        all_scores = []
        for tt, i in units:
            kv = (tt * KVL + i) * KVH // (T * KVL)
            asked = qall[tt, slot, i * R : (i + W) * R, :]
            keys = jnp.concatenate(
                [cache[row, :, (kv + w) * HD : (kv + w + 1) * HD] for w in range(W)], axis=0
            )
            scores = lax.dot_general(asked, keys, NT, preferred_element_type=F32)
            all_scores.append(
                [scores[w * R : (w + 1) * R, w * pos : (w + 1) * pos] * SCALE for w in range(W)]
            )
        all_weights = []
        for (tt, i), scores in zip(units, all_scores):
            rounded = []
            for w in range(W):
                masked = jnp.where(usable, scores[w], NEG_FLOOR)
                highest = jnp.max(masked, axis=1, keepdims=True)
                weights = jnp.where(usable, jnp.exp(masked - highest), 0.0)
                total = jnp.sum(weights, axis=1, keepdims=True)
                rounded.append(weights.astype(BF16))
                stat = jnp.where(lane == tt * SW + i + w, highest, stat)
                stat = jnp.where(lane == tt * SW + KVL + i + w, total, stat)
            all_weights.append(jnp.concatenate(rounded, axis=0))
        for (tt, i), weights in zip(units, all_weights):
            kv = (tt * KVL + i) * KVH // (T * KVL)
            values = cache[row, :, half + kv * HD : half + (kv + W) * HD]
            blended = jnp.dot(weights, values, preferred_element_type=F32)
            for w in range(W):
                obuf[b, tt, i + w, rows, :] = blended[
                    w * R : (w + 1) * R, w * HD : (w + 1) * HD
                ].astype(BF16)
        statbuf[rows, :] = stat

    def send_batch(b):
        turned = statbuf[...].T
        for tt in range(T):
            sbuf[b, tt] = turned[tt * SW : tt * SW + 8, :]
        for n in range(1, T):
            c_st(b, n).start()
            c_o(b, n).start()
        rbuf[b, 0] = obuf[b, t]
        rstat[b, 0] = sbuf[b, t]

    load_res.wait()
    rest = pl.ds(1, T - 1)
    q_rest = qall.at[rest, pl.ds(0, RES_DEV)]
    over_t(q_rest, q_rest, rq_s.at[0], rq_r.at[0], t).wait_recv()

    @pl.loop(0, RES_DEV)
    def _(j):
        attend_slot(res, j, kept[g * RES_DEV + j], j, 0, j)

    send_batch(0)
    load_pre.wait()

    @pl.loop(1, NB)
    def _(b):
        @pl.loop(0, BATCH)
        def _(j):
            k = (b - 1) * BATCH + j
            spread = qall.at[rest, RES_DEV + k]
            over_t(spread, spread, f_s.at[0], f_r.at[k], t).wait_recv()
            source = from_g(k)
            held = tbl[G + source]
            attend_slot(pre, held % MIG_DEV, held // MIG_DEV, RES_DEV + k, b, j)

        send_batch(b)

    def merged(b):
        over_t(rstat.at[b, rest], rstat.at[b, rest], st_s.at[b], st_r.at[b], t).wait_recv()
        over_t(rbuf.at[b, rest], rbuf.at[b, rest], o_s.at[b], o_r.at[b], t).wait_recv()
        tops = [rstat[b, n][:KVL] for n in range(T)]
        highest = functools.reduce(jnp.maximum, tops)
        total = jnp.zeros((KVL, LW), F32)
        for n in range(T):
            factor = jnp.exp(tops[n] - highest)
            total = total + factor * rstat[b, n][KVL:SW]
            facbuf[n * KVL : (n + 1) * KVL, :] = factor
        columns = facbuf[...].T
        blended = []
        for i in range(KVL):
            sum_i = jnp.zeros((LW, HD), F32)
            for n in range(T):
                c = n * KVL + i
                sum_i = sum_i + rbuf[b, n, i].astype(F32) * columns[:, c : c + 1]
            blended.append(sum_i)
        return highest, total, blended

    def finish(b, highest, total, blended, asked):
        r16 = lax.broadcasted_iota(jnp.int32, (BATCH * STEPS, LW), 0)
        lanes = lax.broadcasted_iota(jnp.int32, (BATCH * STEPS, LW), 1)
        causal = (r16 // STEPS == lanes // R) & (r16 % STEPS <= lanes % STEPS)
        adds = []
        for i in range(KVL):
            keys = newk[b, 0, :, i * HD : (i + 1) * HD].astype(BF16)
            values = newk[b, 1, :, i * HD : (i + 1) * HD].astype(BF16)
            scores = lax.dot_general(keys, asked[i], NT, preferred_element_type=F32) * SCALE
            scores = jnp.where(causal, scores, NEG_FLOOR)
            top = jnp.maximum(highest[i : i + 1], jnp.max(scores, axis=0, keepdims=True))
            weights = jnp.where(causal, jnp.exp(scores - top), 0.0)
            carried = jnp.exp(highest[i : i + 1] - top)
            inverse = 1.0 / (total[i : i + 1] * carried + jnp.sum(weights, axis=0, keepdims=True))
            facbuf[i : i + 1, :] = carried
            facbuf[KVL + i : KVL + i + 1, :] = inverse
            adds.append(
                lax.dot_general(weights.astype(BF16), values, TN, preferred_element_type=F32)
            )
        columns = facbuf[...].T
        for i in range(KVL):
            done = blended[i] * columns[:, i : i + 1] + adds[i]
            done = done * columns[:, KVL + i : KVL + i + 1]
            for j in range(BATCH):
                fin[b * BATCH + j, i * R : (i + 1) * R, :] = done[j * R : (j + 1) * R]

    def put(slot, row):
        for h in range(HB):
            piece = fin[slot, h * STEPS : (h + 1) * STEPS, :]
            out[row, :, h * HD : (h + 1) * HD] = piece.astype(BF16)

    for b in range(1, NB):
        highest, total, blended = merged(b)
        packed = jnp.concatenate([highest, total], axis=0)
        zs[b - 1, 0:SW, :] = packed
        for j in range(BATCH):
            k = (b - 1) * BATCH + j
            for i in range(KVL):
                zo[k, i] = blended[i][j * R : (j + 1) * R].astype(BF16)
            if k:
                c_zs(k).start()
                c_zo(k).start()
            else:
                zrs[0] = zs[0]
                zro[0] = zo[0]

    def queries_of(b):
        return [
            jnp.concatenate(
                [
                    (qall[t, j] if b == 0 else zq[(b - 1) * BATCH + j])[i * R : (i + 1) * R]
                    for j in range(BATCH)
                ],
                axis=0,
            )
            for i in range(KVL)
        ]

    finish(0, *merged(0), queries_of(0))
    for j in range(RES_DEV):
        put(j, j)

    for b in range(1, NB):
        lanes = lax.broadcasted_iota(jnp.int32, (8, LW), 1)
        stats = jnp.zeros((8, LW), F32)
        first = (b - 1) * BATCH
        came = pl.ds(max(first, 1), first + BATCH - max(first, 1))
        over_g(zrs.at[came], zrs.at[came], zs_s.at[0], zs_r.at[b - 1], g).wait_recv()
        over_g(zro.at[came], zro.at[came], zo_s.at[0], zo_r.at[b - 1], g).wait_recv()
        for j in range(BATCH):
            k = (b - 1) * BATCH + j
            stats = jnp.where(lanes // R == j, zrs[k], stats)
        blended = [
            jnp.concatenate(
                [zro[(b - 1) * BATCH + j, i].astype(F32) for j in range(BATCH)], axis=0
            )
            for i in range(KVL)
        ]
        finish(b, stats[:KVL], stats[KVL:SW], blended, queries_of(b))
    for l in range(MIG_DEV):
        k_of = 0
        for k in range(1, G):
            k_of = jnp.where(tbl[peer_g(k)] == RES_DEV + l, k, k_of)
        put(RES_DEV + k_of, RES_DEV + l)

    others = pl.ds(1, G - 1)
    over_g(zq.at[others], zq.at[others], zq_s.at[0], zq_r.at[0], g).wait_send()
    over_g(zrs.at[others], zrs.at[others], zs_s.at[0], zs_r.at[0], g).wait_send()
    over_g(zo.at[others], zo.at[others], zo_s.at[0], zo_r.at[0], g).wait_send()
    over_t(q_rest, q_rest, rq_s.at[0], rq_r.at[0], t).wait_send()
    passed = qall.at[0, pl.ds(RES_DEV, G)]
    for n in range(1, T):
        over_t(passed, passed, f_s.at[n], f_r.at[0], t).wait_send()
    for b in range(NB):
        over_t(rstat.at[b, rest], rstat.at[b, rest], st_s.at[b], st_r.at[b], t).wait_send()
        over_t(rbuf.at[b, rest], rbuf.at[b, rest], o_s.at[b], o_r.at[b], t).wait_send()


def routes(kept_tokens, prefill_slot, decode_slot, G):
    g = lax.axis_index("group")
    shape = (2 * G, decode_slot.shape[0])
    n = lax.broadcasted_iota(jnp.int32, shape, 0)
    dest = jnp.broadcast_to(decode_slot[None], shape)
    home = jnp.broadcast_to(prefill_slot[None], shape)
    kept = jnp.broadcast_to(kept_tokens[None], shape)
    dest_group, home_group = dest // PER_GROUP, home // MIG_DEV
    first = n < G
    hit = jnp.where(
        first,
        (dest_group == g) & (home_group == n),
        (home_group == g) & (dest_group == n - G),
    )
    value = jnp.where(
        first, dest - dest_group * PER_GROUP, home - home_group * MIG_DEV + MIG_DEV * kept
    )
    return jnp.sum(jnp.where(hit, value, 0), axis=1)


def body(
    queries,
    new_entries,
    resident_cache,
    prefill_cache,
    resident_kept,
    kept_tokens,
    prefill_slot,
    decode_slot,
):
    G = lax.axis_size("group")
    T = lax.axis_size("tensor")
    KVL = max(1, KVH // T)
    HB = H // T
    RB = STEPS * HB
    R = RB // KVL
    LW = BATCH * R
    NB = 1 + G // BATCH
    tbl = routes(kept_tokens, prefill_slot, decode_slot, G)
    dma = pltpu.SemaphoreType.DMA
    vmem = pl.BlockSpec(memory_space=pltpu.VMEM)
    smem = pl.BlockSpec(memory_space=pltpu.SMEM)
    hbm = pl.BlockSpec(memory_space=pl.ANY)
    return pl.pallas_call(
        functools.partial(kernel, G, T),
        out_shape=jax.ShapeDtypeStruct(queries.shape, BF16),
        in_specs=[smem, smem, vmem, vmem, hbm, hbm],
        out_specs=vmem,
        scratch_shapes=[
            pltpu.VMEM(resident_cache.shape, BF16),
            pltpu.VMEM(prefill_cache.shape, BF16),
            pltpu.VMEM((T, RES_DEV + G, RB, HD), BF16),
            pltpu.VMEM((G, RB, HD), BF16),
            pltpu.VMEM((G + RES_DEV, RB, HD), F32),
            pltpu.VMEM((NB, T, KVL, LW, HD), BF16),
            pltpu.VMEM((NB, T, KVL, LW, HD), BF16),
            pltpu.VMEM((NB, T, 8, LW), F32),
            pltpu.VMEM((NB, T, 8, LW), F32),
            pltpu.VMEM((LW, 128), F32),
            pltpu.VMEM((128, LW), F32),
            pltpu.VMEM((G, KVL, R, HD), BF16),
            pltpu.VMEM((G, KVL, R, HD), BF16),
            pltpu.VMEM((NB - 1, 8, LW), F32),
            pltpu.VMEM((G, 8, LW), F32),
            pltpu.VMEM((NB, 2, BATCH * STEPS, KVL * HD), F32),
            pltpu.VMEM((NB * BATCH, RB, HD), F32),
            dma((2,)),
            dma((1,)),
            dma((G,)),
            dma((1,)),
            dma((1,)),
            dma((T,)),
            dma((G,)),
            dma((NB,)),
            dma((NB,)),
            dma((NB,)),
            dma((NB,)),
            dma((1,)),
            dma((NB - 1,)),
            dma((1,)),
            dma((NB - 1,)),
        ],
        compiler_params=pltpu.CompilerParams(collective_id=0, has_side_effects=True),
    )(tbl, resident_kept, queries, new_entries, resident_cache, prefill_cache)


def solution(mesh):
    in_specs = (
        P("group", None, "tensor"),
        P("group", None, None),
        P("group", "tensor", None),
        P("group", "tensor", None),
        P(),
        P(),
        P(),
        P(),
    )
    out_specs = P("group", None, "tensor")
    return jax.shard_map(body, mesh=mesh, in_specs=in_specs, out_specs=out_specs, check_vma=False)
```

```python
import functools
import math

import jax
import jax.numpy as jnp
from jax import lax
from jax.experimental import pallas as pl
from jax.experimental.pallas import tpu as pltpu
from jax.sharding import PartitionSpec as P

H = 64
KVH = 8
HD = 128
STEPS = 4
MIG_DEV = 8
RES_DEV = 4
PER_GROUP = RES_DEV + MIG_DEV
BATCH = 4

NEG_FLOOR = -1e30
SCALE = 1.0 / math.sqrt(HD)
MESH = pl.DeviceIdType.MESH
F32 = jnp.float32
BF16 = jnp.bfloat16
NT = (((1,), (1,)), ((), ()))
TN = (((0,), (0,)), ((), ()))


def kernel(
    G,
    T,
    tbl,
    kept,
    q_hbm,
    new_hbm,
    res_hbm,
    pre_hbm,
    out,
    q_in,
    new_in,
    res,
    pre,
    qall,
    zq,
    stage,
    obuf,
    rbuf,
    sbuf,
    rstat,
    statbuf,
    facbuf,
    zo,
    zro,
    zs,
    zrs,
    newk,
    nstat,
    nadd,
    fin,
    cache_sem,
    zq_s,
    zq_r,
    rq_s,
    rq_r,
    f_s,
    f_r,
    o_s,
    o_r,
    st_s,
    st_r,
    zo_s,
    zo_r,
    zs_s,
    zs_r,
):
    KVL = max(1, KVH // T)
    HB = H // T
    HU = HB // KVL
    R = STEPS * HU
    LW = BATCH * R
    SW = 2 * KVL
    NB = 1 + G // BATCH
    pos = res.shape[1]
    half = KVH * HD
    g = lax.axis_index("group")
    t = lax.axis_index("tensor")
    offset = t * pos

    def peer_t(k):
        return lax.rem(t + k, T)

    def peer_g(k):
        return lax.rem(g + k, G)

    def from_g(k):
        return lax.rem(g - k + G, G)

    def over_t(src, dst, ssem, rsem, dev):
        return pltpu.make_async_remote_copy(
            src_ref=src, dst_ref=dst, send_sem=ssem, recv_sem=rsem,
            device_id=(g, dev), device_id_type=MESH,
        )

    def over_g(src, dst, ssem, rsem, dev):
        return pltpu.make_async_remote_copy(
            src_ref=src, dst_ref=dst, send_sem=ssem, recv_sem=rsem,
            device_id=(dev, t), device_id_type=MESH,
        )

    def c_zq(k):
        return over_g(zq.at[k], qall.at[t, RES_DEV + k], zq_s.at[0], zq_r.at[k], peer_g(k))

    def c_rq(k):
        p = peer_t(k)
        own = qall.at[t, pl.ds(0, RES_DEV)]
        return over_t(own, own, rq_s.at[0], rq_r.at[0], p)

    def c_fwd(k, n):
        own = qall.at[t, RES_DEV + k]
        return over_t(own, own, f_s.at[n], f_r.at[k], peer_t(n))

    def c_o(b, n):
        p = peer_t(n)
        return over_t(obuf.at[b, p], rbuf.at[b, n], o_s.at[b], o_r.at[b], p)

    def c_st(b, n):
        p = peer_t(n)
        return over_t(sbuf.at[b, p], rstat.at[b, n], st_s.at[b], st_r.at[b], p)

    def c_zo(k):
        return over_g(zo.at[k], zro.at[k], zo_s.at[0], zo_r.at[k // BATCH], from_g(k))

    def c_zs(k):
        return over_g(zs.at[k // BATCH], zrs.at[k], zs_s.at[0], zs_r.at[k // BATCH], from_g(k))

    barrier = pltpu.get_barrier_semaphore()
    for k in range(G - 1, 0, -1):
        pl.semaphore_signal(barrier, inc=1, device_id=(peer_g(k), t), device_id_type=MESH)
    for k in range(1, T):
        pl.semaphore_signal(barrier, inc=1, device_id=(g, peer_t(k)), device_id_type=MESH)
    load_q = pltpu.make_async_copy(q_hbm, q_in, cache_sem.at[2])
    load_new = pltpu.make_async_copy(new_hbm, new_in, cache_sem.at[3])
    load_res = pltpu.make_async_copy(res_hbm, res, cache_sem.at[0])
    load_pre = pltpu.make_async_copy(pre_hbm, pre, cache_sem.at[1])
    load_q.start()
    load_new.start()
    load_pre.start()
    load_res.start()
    load_q.wait()

    def arranged(row, slot):
        for h in range(HB):
            piece = q_in[row, :, h * HD : (h + 1) * HD]
            stage[slot, h * STEPS : (h + 1) * STEPS, :] = piece.astype(F32)
        return stage[slot].astype(BF16)

    for k in range(G):
        block = arranged(tbl[peer_g(k)], k)
        zq[k] = block
        if k == 0:
            qall[t, RES_DEV] = block
    for j in range(RES_DEV):
        qall[t, j] = arranged(j, G + j)

    pl.semaphore_wait(barrier, G - 1 + T - 1)
    for k in range(1, G):
        c_zq(k).start()
    for n in range(1, T):
        c_rq(n).start()
    for n in range(1, T):
        c_fwd(0, n).start()

    load_new.wait()
    kv_col = pl.multiple_of((t * KVL * KVH) // (T * KVL) * HD, HD)
    for b in range(NB):
        for j in range(BATCH):
            row = j if b == 0 else tbl[peer_g((b - 1) * BATCH + j)]
            lo = j * STEPS
            newk[b, 0, lo : lo + STEPS, :] = new_in[row, :, pl.ds(kv_col, KVL * HD)].astype(F32)
            newk[b, 1, lo : lo + STEPS, :] = new_in[
                row, :, pl.ds(pl.multiple_of(half + kv_col, HD), KVL * HD)
            ].astype(F32)

    def queries_of(b):
        return [
            jnp.concatenate(
                [
                    (qall[t, j] if b == 0 else zq[(b - 1) * BATCH + j])[i * R : (i + 1) * R]
                    for j in range(BATCH)
                ],
                axis=0,
            )
            for i in range(KVL)
        ]

    r16 = lax.broadcasted_iota(jnp.int32, (BATCH * STEPS, LW), 0)
    lanes16 = lax.broadcasted_iota(jnp.int32, (BATCH * STEPS, LW), 1)
    causal = (r16 // STEPS == lanes16 // R) & (r16 % STEPS <= lanes16 % STEPS)
    for b in range(NB):
        asked_b = queries_of(b)
        for i in range(KVL):
            keys = newk[b, 0, :, i * HD : (i + 1) * HD].astype(BF16)
            values = newk[b, 1, :, i * HD : (i + 1) * HD].astype(BF16)
            scores = lax.dot_general(keys, asked_b[i], NT, preferred_element_type=F32) * SCALE
            scores = jnp.where(causal, scores, NEG_FLOOR)
            top = jnp.max(scores, axis=0, keepdims=True)
            weights = jnp.where(causal, jnp.exp(scores - top), 0.0)
            nstat[b, i : i + 1, :] = top
            nstat[b, KVL + i : KVL + i + 1, :] = jnp.sum(weights, axis=0, keepdims=True)
            nadd[b, i] = lax.dot_general(
                weights.astype(BF16), values, TN, preferred_element_type=F32
            )

    for k in range(1, G):
        c_zq(k).wait_recv()
        for n in range(1, T):
            c_fwd(k, n).start()

    def attend_slot(cache, row, length, slot, b, j):
        lane = lax.broadcasted_iota(jnp.int32, (R, 128), 1)
        usable = offset + lax.broadcasted_iota(jnp.int32, (R, pos), 1) < length
        stat = jnp.zeros((R, 128), F32)
        rows = pl.ds(pl.multiple_of(j * R, R), R)
        W = 2 if KVL % 2 == 0 else 1
        units = [(tt, i) for tt in range(T) for i in range(0, KVL, W)]
        all_scores = []
        for tt, i in units:
            kv = (tt * KVL + i) * KVH // (T * KVL)
            asked = qall[tt, slot, i * R : (i + W) * R, :]
            keys = jnp.concatenate(
                [cache[row, :, (kv + w) * HD : (kv + w + 1) * HD] for w in range(W)], axis=0
            )
            scores = lax.dot_general(asked, keys, NT, preferred_element_type=F32)
            all_scores.append(
                [scores[w * R : (w + 1) * R, w * pos : (w + 1) * pos] * SCALE for w in range(W)]
            )
        all_weights = []
        for (tt, i), scores in zip(units, all_scores):
            rounded = []
            for w in range(W):
                masked = jnp.where(usable, scores[w], NEG_FLOOR)
                highest = jnp.max(masked, axis=1, keepdims=True)
                weights = jnp.where(usable, jnp.exp(masked - highest), 0.0)
                total = jnp.sum(weights, axis=1, keepdims=True)
                rounded.append(weights.astype(BF16))
                stat = jnp.where(lane == tt * SW + i + w, highest, stat)
                stat = jnp.where(lane == tt * SW + KVL + i + w, total, stat)
            all_weights.append(jnp.concatenate(rounded, axis=0))
        for (tt, i), weights in zip(units, all_weights):
            kv = (tt * KVL + i) * KVH // (T * KVL)
            values = cache[row, :, half + kv * HD : half + (kv + W) * HD]
            blended = jnp.dot(weights, values, preferred_element_type=F32)
            for w in range(W):
                obuf[b, tt, i + w, rows, :] = blended[
                    w * R : (w + 1) * R, w * HD : (w + 1) * HD
                ].astype(BF16)
        statbuf[rows, :] = stat

    def send_batch(b):
        turned = statbuf[...].T
        for tt in range(T):
            sbuf[b, tt] = turned[tt * SW : tt * SW + 8, :]
        for n in range(1, T):
            c_st(b, n).start()
            c_o(b, n).start()
        rbuf[b, 0] = obuf[b, t]
        rstat[b, 0] = sbuf[b, t]

    rest = pl.ds(1, T - 1)
    load_pre.wait()

    @pl.loop(1, NB)
    def _(b):
        @pl.loop(0, BATCH)
        def _(j):
            k = (b - 1) * BATCH + j
            spread = qall.at[rest, RES_DEV + k]
            over_t(spread, spread, f_s.at[0], f_r.at[k], t).wait_recv()
            source = from_g(k)
            held = tbl[G + source]
            attend_slot(pre, held % MIG_DEV, held // MIG_DEV, RES_DEV + k, b, j)

        send_batch(b)

    load_res.wait()
    q_rest = qall.at[rest, pl.ds(0, RES_DEV)]
    over_t(q_rest, q_rest, rq_s.at[0], rq_r.at[0], t).wait_recv()

    @pl.loop(0, RES_DEV)
    def _(j):
        attend_slot(res, j, kept[g * RES_DEV + j], j, 0, j)

    send_batch(0)
    def merged(b):
        over_t(rstat.at[b, rest], rstat.at[b, rest], st_s.at[b], st_r.at[b], t).wait_recv()
        over_t(rbuf.at[b, rest], rbuf.at[b, rest], o_s.at[b], o_r.at[b], t).wait_recv()
        tops = [rstat[b, n][:KVL] for n in range(T)]
        highest = functools.reduce(jnp.maximum, tops)
        total = jnp.zeros((KVL, LW), F32)
        for n in range(T):
            factor = jnp.exp(tops[n] - highest)
            total = total + factor * rstat[b, n][KVL:SW]
            facbuf[n * KVL : (n + 1) * KVL, :] = factor
        columns = facbuf[...].T
        blended = []
        for i in range(KVL):
            sum_i = jnp.zeros((LW, HD), F32)
            for n in range(T):
                c = n * KVL + i
                sum_i = sum_i + rbuf[b, n, i].astype(F32) * columns[:, c : c + 1]
            blended.append(sum_i)
        return highest, total, blended

    def finish(b, highest, total, blended):
        new_top, new_total = nstat[b, 0:KVL], nstat[b, KVL:SW]
        top = jnp.maximum(highest, new_top)
        old_part, new_part = jnp.exp(highest - top), jnp.exp(new_top - top)
        inverse = 1.0 / (total * old_part + new_total * new_part)
        facbuf[0:KVL, :] = old_part * inverse
        facbuf[KVL:SW, :] = new_part * inverse
        columns = facbuf[...].T
        for i in range(KVL):
            done = blended[i] * columns[:, i : i + 1]
            done = done + nadd[b, i] * columns[:, KVL + i : KVL + i + 1]
            for j in range(BATCH):
                fin[b * BATCH + j, i * R : (i + 1) * R, :] = done[j * R : (j + 1) * R]

    def put(slot, row):
        for h in range(HB):
            piece = fin[slot, h * STEPS : (h + 1) * STEPS, :]
            out[row, :, h * HD : (h + 1) * HD] = piece.astype(BF16)

    for b in range(1, NB):
        highest, total, blended = merged(b)
        packed = jnp.concatenate([highest, total], axis=0)
        zs[b - 1, 0:SW, :] = packed
        for j in range(BATCH):
            k = (b - 1) * BATCH + j
            for i in range(KVL):
                zo[k, i] = blended[i][j * R : (j + 1) * R].astype(BF16)
            if k:
                c_zs(k).start()
                c_zo(k).start()
            else:
                zrs[0] = zs[0]
                zro[0] = zo[0]

    finish(0, *merged(0))
    for j in range(RES_DEV):
        put(j, j)

    for b in range(1, NB):
        lanes = lax.broadcasted_iota(jnp.int32, (8, LW), 1)
        stats = jnp.zeros((8, LW), F32)
        first = (b - 1) * BATCH
        came = pl.ds(max(first, 1), first + BATCH - max(first, 1))
        over_g(zrs.at[came], zrs.at[came], zs_s.at[0], zs_r.at[b - 1], g).wait_recv()
        over_g(zro.at[came], zro.at[came], zo_s.at[0], zo_r.at[b - 1], g).wait_recv()
        for j in range(BATCH):
            k = (b - 1) * BATCH + j
            stats = jnp.where(lanes // R == j, zrs[k], stats)
        blended = [
            jnp.concatenate(
                [zro[(b - 1) * BATCH + j, i].astype(F32) for j in range(BATCH)], axis=0
            )
            for i in range(KVL)
        ]
        finish(b, stats[:KVL], stats[KVL:SW], blended)
    for l in range(MIG_DEV):
        k_of = 0
        for k in range(1, G):
            k_of = jnp.where(tbl[peer_g(k)] == RES_DEV + l, k, k_of)
        put(RES_DEV + k_of, RES_DEV + l)

    others = pl.ds(1, G - 1)
    over_g(zq.at[others], zq.at[others], zq_s.at[0], zq_r.at[0], g).wait_send()
    over_g(zrs.at[others], zrs.at[others], zs_s.at[0], zs_r.at[0], g).wait_send()
    over_g(zo.at[others], zo.at[others], zo_s.at[0], zo_r.at[0], g).wait_send()
    over_t(q_rest, q_rest, rq_s.at[0], rq_r.at[0], t).wait_send()
    passed = qall.at[0, pl.ds(RES_DEV, G)]
    for n in range(1, T):
        over_t(passed, passed, f_s.at[n], f_r.at[0], t).wait_send()
    for b in range(NB):
        over_t(rstat.at[b, rest], rstat.at[b, rest], st_s.at[b], st_r.at[b], t).wait_send()
        over_t(rbuf.at[b, rest], rbuf.at[b, rest], o_s.at[b], o_r.at[b], t).wait_send()


def routes(kept_tokens, prefill_slot, decode_slot, G):
    g = lax.axis_index("group")
    shape = (2 * G, decode_slot.shape[0])
    n = lax.broadcasted_iota(jnp.int32, shape, 0)
    dest = jnp.broadcast_to(decode_slot[None], shape)
    home = jnp.broadcast_to(prefill_slot[None], shape)
    kept = jnp.broadcast_to(kept_tokens[None], shape)
    dest_group, home_group = dest // PER_GROUP, home // MIG_DEV
    first = n < G
    hit = jnp.where(
        first,
        (dest_group == g) & (home_group == n),
        (home_group == g) & (dest_group == n - G),
    )
    value = jnp.where(
        first, dest - dest_group * PER_GROUP, home - home_group * MIG_DEV + MIG_DEV * kept
    )
    return jnp.sum(jnp.where(hit, value, 0), axis=1)


def body(
    queries,
    new_entries,
    resident_cache,
    prefill_cache,
    resident_kept,
    kept_tokens,
    prefill_slot,
    decode_slot,
):
    G = lax.axis_size("group")
    T = lax.axis_size("tensor")
    KVL = max(1, KVH // T)
    HB = H // T
    RB = STEPS * HB
    R = RB // KVL
    LW = BATCH * R
    NB = 1 + G // BATCH
    tbl = routes(kept_tokens, prefill_slot, decode_slot, G)
    dma = pltpu.SemaphoreType.DMA
    vmem = pl.BlockSpec(memory_space=pltpu.VMEM)
    smem = pl.BlockSpec(memory_space=pltpu.SMEM)
    hbm = pl.BlockSpec(memory_space=pl.ANY)
    return pl.pallas_call(
        functools.partial(kernel, G, T),
        out_shape=pltpu.VMEM(queries.shape, BF16),
        in_specs=[smem, smem, hbm, hbm, hbm, hbm],
        out_specs=vmem,
        scratch_shapes=[
            pltpu.VMEM(queries.shape, BF16),
            pltpu.VMEM(new_entries.shape, BF16),
            pltpu.VMEM(resident_cache.shape, BF16),
            pltpu.VMEM(prefill_cache.shape, BF16),
            pltpu.VMEM((T, RES_DEV + G, RB, HD), BF16),
            pltpu.VMEM((G, RB, HD), BF16),
            pltpu.VMEM((G + RES_DEV, RB, HD), F32),
            pltpu.VMEM((NB, T, KVL, LW, HD), BF16),
            pltpu.VMEM((NB, T, KVL, LW, HD), BF16),
            pltpu.VMEM((NB, T, 8, LW), F32),
            pltpu.VMEM((NB, T, 8, LW), F32),
            pltpu.VMEM((LW, 128), F32),
            pltpu.VMEM((128, LW), F32),
            pltpu.VMEM((G, KVL, R, HD), BF16),
            pltpu.VMEM((G, KVL, R, HD), BF16),
            pltpu.VMEM((NB - 1, 8, LW), F32),
            pltpu.VMEM((G, 8, LW), F32),
            pltpu.VMEM((NB, 2, BATCH * STEPS, KVL * HD), F32),
            pltpu.VMEM((NB, 8, LW), F32),
            pltpu.VMEM((NB, KVL, LW, HD), F32),
            pltpu.VMEM((NB * BATCH, RB, HD), F32),
            dma((4,)),
            dma((1,)),
            dma((G,)),
            dma((1,)),
            dma((1,)),
            dma((T,)),
            dma((G,)),
            dma((NB,)),
            dma((NB,)),
            dma((NB,)),
            dma((NB,)),
            dma((1,)),
            dma((NB - 1,)),
            dma((1,)),
            dma((NB - 1,)),
        ],
        compiler_params=pltpu.CompilerParams(collective_id=0, has_side_effects=True),
    )(tbl, resident_kept, queries, new_entries, resident_cache, prefill_cache)


def solution(mesh):
    in_specs = (
        P("group", None, "tensor"),
        P("group", None, None),
        P("group", "tensor", None),
        P("group", "tensor", None),
        P(),
        P(),
        P(),
        P(),
    )
    out_specs = P("group", None, "tensor")
    return jax.shard_map(body, mesh=mesh, in_specs=in_specs, out_specs=out_specs, check_vma=False)
```

```python
import functools
import math

import jax
import jax.numpy as jnp
from jax import lax
from jax.experimental import pallas as pl
from jax.experimental.pallas import tpu as pltpu
from jax.sharding import PartitionSpec as P

H = 64
KVH = 8
HD = 128
STEPS = 4
MIG_DEV = 8
RES_DEV = 4
PER_GROUP = RES_DEV + MIG_DEV
BATCH = 4

NEG_FLOOR = -1e30
SCALE = 1.0 / math.sqrt(HD)
MESH = pl.DeviceIdType.MESH
F32 = jnp.float32
BF16 = jnp.bfloat16
NT = (((1,), (1,)), ((), ()))
TN = (((0,), (0,)), ((), ()))


def fill_table(G, g, kept_v, home_v, dest_v, tab_v):
    shape = (2 * G, dest_v.shape[1])
    n = lax.broadcasted_iota(jnp.int32, shape, 0)
    dest = jnp.broadcast_to(dest_v[...], shape)
    home = jnp.broadcast_to(home_v[...], shape)
    kept = jnp.broadcast_to(kept_v[...], shape)
    dest_group, home_group = lax.div(dest, PER_GROUP), lax.div(home, MIG_DEV)
    arriving = (dest_group == g) & (home_group == n)
    leaving = (home_group == g) & (dest_group == n - G)
    picked = jnp.where(arriving, dest - dest_group * PER_GROUP, 0)
    held = home - home_group * MIG_DEV + MIG_DEV * kept
    picked = picked + jnp.where(leaving, held, 0)
    total = jnp.sum(picked, axis=1, keepdims=True)
    tab_v[...] = jnp.broadcast_to(total, tab_v.shape)


def kernel(
    G,
    T,
    kept_v,
    home_v,
    dest_v,
    kept,
    q_hbm,
    new_hbm,
    res_hbm,
    pre_hbm,
    out,
    tab_v,
    tab_s,
    q_in,
    new_in,
    res,
    pre,
    qall,
    zq,
    stage,
    obuf,
    rbuf,
    sbuf,
    rstat,
    statbuf,
    facbuf,
    zo,
    zro,
    zs,
    zrs,
    newk,
    nstat,
    nadd,
    fin,
    cache_sem,
    zq_s,
    zq_r,
    rq_s,
    rq_r,
    f_s,
    f_r,
    o_s,
    o_r,
    st_s,
    st_r,
    zo_s,
    zo_r,
    zs_s,
    zs_r,
):
    KVL = max(1, KVH // T)
    HB = H // T
    HU = HB // KVL
    R = STEPS * HU
    LW = BATCH * R
    SW = 2 * KVL
    NB = 1 + G // BATCH
    pos = res.shape[1]
    half = KVH * HD
    g = lax.axis_index("group")
    t = lax.axis_index("tensor")
    offset = t * pos

    def peer_t(k):
        return lax.rem(t + k, T)

    def peer_g(k):
        return lax.rem(g + k, G)

    def from_g(k):
        return lax.rem(g - k + G, G)

    def over_t(src, dst, ssem, rsem, dev):
        return pltpu.make_async_remote_copy(
            src_ref=src, dst_ref=dst, send_sem=ssem, recv_sem=rsem,
            device_id=(g, dev), device_id_type=MESH,
        )

    def over_g(src, dst, ssem, rsem, dev):
        return pltpu.make_async_remote_copy(
            src_ref=src, dst_ref=dst, send_sem=ssem, recv_sem=rsem,
            device_id=(dev, t), device_id_type=MESH,
        )

    def c_zq(k):
        return over_g(zq.at[k], qall.at[t, RES_DEV + k], zq_s.at[0], zq_r.at[k], peer_g(k))

    def c_rq(k):
        p = peer_t(k)
        own = qall.at[t, pl.ds(0, RES_DEV)]
        return over_t(own, own, rq_s.at[0], rq_r.at[0], p)

    def c_fwd(k, n):
        own = qall.at[t, RES_DEV + k]
        return over_t(own, own, f_s.at[n], f_r.at[k], peer_t(n))

    def c_o(b, n):
        p = peer_t(n)
        return over_t(obuf.at[b, p], rbuf.at[b, n], o_s.at[b], o_r.at[b], p)

    def c_st(b, n):
        p = peer_t(n)
        return over_t(sbuf.at[b, p], rstat.at[b, n], st_s.at[b], st_r.at[b], p)

    def c_zo(k):
        return over_g(zo.at[k], zro.at[k], zo_s.at[0], zo_r.at[k // BATCH], from_g(k))

    def c_zs(k):
        return over_g(zs.at[k // BATCH], zrs.at[k], zs_s.at[0], zs_r.at[k // BATCH], from_g(k))

    barrier = pltpu.get_barrier_semaphore()
    for k in range(G - 1, 0, -1):
        pl.semaphore_signal(barrier, inc=1, device_id=(peer_g(k), t), device_id_type=MESH)
    for k in range(1, T):
        pl.semaphore_signal(barrier, inc=1, device_id=(g, peer_t(k)), device_id_type=MESH)
    load_q = pltpu.make_async_copy(q_hbm, q_in, cache_sem.at[2])
    load_new = pltpu.make_async_copy(new_hbm, new_in, cache_sem.at[3])
    load_res = pltpu.make_async_copy(res_hbm, res, cache_sem.at[0])
    load_pre = pltpu.make_async_copy(pre_hbm, pre, cache_sem.at[1])
    load_q.start()
    load_new.start()
    load_pre.start()
    load_res.start()
    fill_table(G, g, kept_v, home_v, dest_v, tab_v)
    load_tab = pltpu.make_async_copy(tab_v, tab_s, cache_sem.at[4])
    load_tab.start()
    load_tab.wait()
    load_q.wait()

    def arranged(row, slot):
        for h in range(HB):
            piece = q_in[row, :, h * HD : (h + 1) * HD]
            stage[slot, h * STEPS : (h + 1) * STEPS, :] = piece.astype(F32)
        return stage[slot].astype(BF16)

    for k in range(G):
        block = arranged(tab_s[peer_g(k), 0], k)
        zq[k] = block
        if k == 0:
            qall[t, RES_DEV] = block
    for j in range(RES_DEV):
        qall[t, j] = arranged(j, G + j)

    pl.semaphore_wait(barrier, G - 1 + T - 1)
    for k in range(1, G):
        c_zq(k).start()
    for n in range(1, T):
        c_rq(n).start()
    for n in range(1, T):
        c_fwd(0, n).start()

    load_new.wait()
    kv_col = pl.multiple_of((t * KVL * KVH) // (T * KVL) * HD, HD)
    for b in range(NB):
        for j in range(BATCH):
            row = j if b == 0 else tab_s[peer_g((b - 1) * BATCH + j), 0]
            lo = j * STEPS
            newk[b, 0, lo : lo + STEPS, :] = new_in[row, :, pl.ds(kv_col, KVL * HD)].astype(F32)
            newk[b, 1, lo : lo + STEPS, :] = new_in[
                row, :, pl.ds(pl.multiple_of(half + kv_col, HD), KVL * HD)
            ].astype(F32)

    def queries_of(b):
        return [
            jnp.concatenate(
                [
                    (qall[t, j] if b == 0 else zq[(b - 1) * BATCH + j])[i * R : (i + 1) * R]
                    for j in range(BATCH)
                ],
                axis=0,
            )
            for i in range(KVL)
        ]

    r16 = lax.broadcasted_iota(jnp.int32, (BATCH * STEPS, LW), 0)
    lanes16 = lax.broadcasted_iota(jnp.int32, (BATCH * STEPS, LW), 1)
    causal = (r16 // STEPS == lanes16 // R) & (r16 % STEPS <= lanes16 % STEPS)
    for b in range(NB):
        asked_b = queries_of(b)
        for i in range(KVL):
            keys = newk[b, 0, :, i * HD : (i + 1) * HD].astype(BF16)
            values = newk[b, 1, :, i * HD : (i + 1) * HD].astype(BF16)
            scores = lax.dot_general(keys, asked_b[i], NT, preferred_element_type=F32) * SCALE
            scores = jnp.where(causal, scores, NEG_FLOOR)
            top = jnp.max(scores, axis=0, keepdims=True)
            weights = jnp.where(causal, jnp.exp(scores - top), 0.0)
            nstat[b, i : i + 1, :] = top
            nstat[b, KVL + i : KVL + i + 1, :] = jnp.sum(weights, axis=0, keepdims=True)
            nadd[b, i] = lax.dot_general(
                weights.astype(BF16), values, TN, preferred_element_type=F32
            )

    for k in range(1, G):
        c_zq(k).wait_recv()
        for n in range(1, T):
            c_fwd(k, n).start()

    def attend_slot(cache, row, length, slot, b, j):
        lane = lax.broadcasted_iota(jnp.int32, (R, 128), 1)
        usable = offset + lax.broadcasted_iota(jnp.int32, (R, pos), 1) < length
        stat = jnp.zeros((R, 128), F32)
        rows = pl.ds(pl.multiple_of(j * R, R), R)
        W = 2 if KVL % 2 == 0 else 1
        units = [(tt, i) for tt in range(T) for i in range(0, KVL, W)]
        all_scores = []
        for tt, i in units:
            kv = (tt * KVL + i) * KVH // (T * KVL)
            asked = qall[tt, slot, i * R : (i + W) * R, :]
            keys = jnp.concatenate(
                [cache[row, :, (kv + w) * HD : (kv + w + 1) * HD] for w in range(W)], axis=0
            )
            scores = lax.dot_general(asked, keys, NT, preferred_element_type=F32)
            all_scores.append(
                [scores[w * R : (w + 1) * R, w * pos : (w + 1) * pos] * SCALE for w in range(W)]
            )
        all_weights = []
        for (tt, i), scores in zip(units, all_scores):
            rounded = []
            for w in range(W):
                masked = jnp.where(usable, scores[w], NEG_FLOOR)
                highest = jnp.max(masked, axis=1, keepdims=True)
                weights = jnp.where(usable, jnp.exp(masked - highest), 0.0)
                total = jnp.sum(weights, axis=1, keepdims=True)
                rounded.append(weights.astype(BF16))
                stat = jnp.where(lane == tt * SW + i + w, highest, stat)
                stat = jnp.where(lane == tt * SW + KVL + i + w, total, stat)
            all_weights.append(jnp.concatenate(rounded, axis=0))
        for (tt, i), weights in zip(units, all_weights):
            kv = (tt * KVL + i) * KVH // (T * KVL)
            values = cache[row, :, half + kv * HD : half + (kv + W) * HD]
            blended = jnp.dot(weights, values, preferred_element_type=F32)
            for w in range(W):
                obuf[b, tt, i + w, rows, :] = blended[
                    w * R : (w + 1) * R, w * HD : (w + 1) * HD
                ].astype(BF16)
        statbuf[rows, :] = stat

    def send_batch(b):
        turned = statbuf[...].T
        for tt in range(T):
            sbuf[b, tt] = turned[tt * SW : tt * SW + 8, :]
        for n in range(1, T):
            c_st(b, n).start()
            c_o(b, n).start()
        rbuf[b, 0] = obuf[b, t]
        rstat[b, 0] = sbuf[b, t]

    rest = pl.ds(1, T - 1)
    load_pre.wait()

    @pl.loop(1, NB)
    def _(b):
        @pl.loop(0, BATCH)
        def _(j):
            k = (b - 1) * BATCH + j
            spread = qall.at[rest, RES_DEV + k]
            over_t(spread, spread, f_s.at[0], f_r.at[k], t).wait_recv()
            source = from_g(k)
            held = tab_s[G + source, 0]
            attend_slot(pre, held % MIG_DEV, held // MIG_DEV, RES_DEV + k, b, j)

        send_batch(b)

    load_res.wait()
    q_rest = qall.at[rest, pl.ds(0, RES_DEV)]
    over_t(q_rest, q_rest, rq_s.at[0], rq_r.at[0], t).wait_recv()

    @pl.loop(0, RES_DEV)
    def _(j):
        attend_slot(res, j, kept[g * RES_DEV + j], j, 0, j)

    send_batch(0)
    def merged(b):
        over_t(rstat.at[b, rest], rstat.at[b, rest], st_s.at[b], st_r.at[b], t).wait_recv()
        over_t(rbuf.at[b, rest], rbuf.at[b, rest], o_s.at[b], o_r.at[b], t).wait_recv()
        tops = [rstat[b, n][:KVL] for n in range(T)]
        highest = functools.reduce(jnp.maximum, tops)
        total = jnp.zeros((KVL, LW), F32)
        for n in range(T):
            factor = jnp.exp(tops[n] - highest)
            total = total + factor * rstat[b, n][KVL:SW]
            facbuf[n * KVL : (n + 1) * KVL, :] = factor
        columns = facbuf[...].T
        blended = []
        for i in range(KVL):
            sum_i = jnp.zeros((LW, HD), F32)
            for n in range(T):
                c = n * KVL + i
                sum_i = sum_i + rbuf[b, n, i].astype(F32) * columns[:, c : c + 1]
            blended.append(sum_i)
        return highest, total, blended

    def finish(b, highest, total, blended):
        new_top, new_total = nstat[b, 0:KVL], nstat[b, KVL:SW]
        top = jnp.maximum(highest, new_top)
        old_part, new_part = jnp.exp(highest - top), jnp.exp(new_top - top)
        inverse = 1.0 / (total * old_part + new_total * new_part)
        facbuf[0:KVL, :] = old_part * inverse
        facbuf[KVL:SW, :] = new_part * inverse
        columns = facbuf[...].T
        for i in range(KVL):
            done = blended[i] * columns[:, i : i + 1]
            done = done + nadd[b, i] * columns[:, KVL + i : KVL + i + 1]
            for j in range(BATCH):
                fin[b * BATCH + j, i * R : (i + 1) * R, :] = done[j * R : (j + 1) * R]

    def put(slot, row):
        for h in range(HB):
            piece = fin[slot, h * STEPS : (h + 1) * STEPS, :]
            out[row, :, h * HD : (h + 1) * HD] = piece.astype(BF16)

    for b in range(1, NB):
        highest, total, blended = merged(b)
        packed = jnp.concatenate([highest, total], axis=0)
        zs[b - 1, 0:SW, :] = packed
        for j in range(BATCH):
            k = (b - 1) * BATCH + j
            for i in range(KVL):
                zo[k, i] = blended[i][j * R : (j + 1) * R].astype(BF16)
            if k:
                c_zs(k).start()
                c_zo(k).start()
            else:
                zrs[0] = zs[0]
                zro[0] = zo[0]

    finish(0, *merged(0))
    for j in range(RES_DEV):
        put(j, j)

    for b in range(1, NB):
        lanes = lax.broadcasted_iota(jnp.int32, (8, LW), 1)
        stats = jnp.zeros((8, LW), F32)
        first = (b - 1) * BATCH
        came = pl.ds(max(first, 1), first + BATCH - max(first, 1))
        over_g(zrs.at[came], zrs.at[came], zs_s.at[0], zs_r.at[b - 1], g).wait_recv()
        over_g(zro.at[came], zro.at[came], zo_s.at[0], zo_r.at[b - 1], g).wait_recv()
        for j in range(BATCH):
            k = (b - 1) * BATCH + j
            stats = jnp.where(lanes // R == j, zrs[k], stats)
        blended = [
            jnp.concatenate(
                [zro[(b - 1) * BATCH + j, i].astype(F32) for j in range(BATCH)], axis=0
            )
            for i in range(KVL)
        ]
        finish(b, stats[:KVL], stats[KVL:SW], blended)
    for l in range(MIG_DEV):
        k_of = 0
        for k in range(1, G):
            k_of = jnp.where(tab_s[peer_g(k), 0] == RES_DEV + l, k, k_of)
        put(RES_DEV + k_of, RES_DEV + l)

    others = pl.ds(1, G - 1)
    over_g(zq.at[others], zq.at[others], zq_s.at[0], zq_r.at[0], g).wait_send()
    over_g(zrs.at[others], zrs.at[others], zs_s.at[0], zs_r.at[0], g).wait_send()
    over_g(zo.at[others], zo.at[others], zo_s.at[0], zo_r.at[0], g).wait_send()
    over_t(q_rest, q_rest, rq_s.at[0], rq_r.at[0], t).wait_send()
    passed = qall.at[0, pl.ds(RES_DEV, G)]
    for n in range(1, T):
        over_t(passed, passed, f_s.at[n], f_r.at[0], t).wait_send()
    for b in range(NB):
        over_t(rstat.at[b, rest], rstat.at[b, rest], st_s.at[b], st_r.at[b], t).wait_send()
        over_t(rbuf.at[b, rest], rbuf.at[b, rest], o_s.at[b], o_r.at[b], t).wait_send()


def body(
    queries,
    new_entries,
    resident_cache,
    prefill_cache,
    resident_kept,
    kept_tokens,
    prefill_slot,
    decode_slot,
):
    G = lax.axis_size("group")
    T = lax.axis_size("tensor")
    KVL = max(1, KVH // T)
    HB = H // T
    RB = STEPS * HB
    R = RB // KVL
    LW = BATCH * R
    NB = 1 + G // BATCH
    dma = pltpu.SemaphoreType.DMA
    vmem = pl.BlockSpec(memory_space=pltpu.VMEM)
    smem = pl.BlockSpec(memory_space=pltpu.SMEM)
    hbm = pl.BlockSpec(memory_space=pl.ANY)
    return pl.pallas_call(
        functools.partial(kernel, G, T),
        out_shape=pltpu.VMEM(queries.shape, BF16),
        in_specs=[vmem, vmem, vmem, smem, hbm, hbm, hbm, hbm],
        out_specs=vmem,
        scratch_shapes=[
            pltpu.VMEM((2 * G, 128), jnp.int32),
            pltpu.SMEM((2 * G, 128), jnp.int32),
            pltpu.VMEM(queries.shape, BF16),
            pltpu.VMEM(new_entries.shape, BF16),
            pltpu.VMEM(resident_cache.shape, BF16),
            pltpu.VMEM(prefill_cache.shape, BF16),
            pltpu.VMEM((T, RES_DEV + G, RB, HD), BF16),
            pltpu.VMEM((G, RB, HD), BF16),
            pltpu.VMEM((G + RES_DEV, RB, HD), F32),
            pltpu.VMEM((NB, T, KVL, LW, HD), BF16),
            pltpu.VMEM((NB, T, KVL, LW, HD), BF16),
            pltpu.VMEM((NB, T, 8, LW), F32),
            pltpu.VMEM((NB, T, 8, LW), F32),
            pltpu.VMEM((LW, 128), F32),
            pltpu.VMEM((128, LW), F32),
            pltpu.VMEM((G, KVL, R, HD), BF16),
            pltpu.VMEM((G, KVL, R, HD), BF16),
            pltpu.VMEM((NB - 1, 8, LW), F32),
            pltpu.VMEM((G, 8, LW), F32),
            pltpu.VMEM((NB, 2, BATCH * STEPS, KVL * HD), F32),
            pltpu.VMEM((NB, 8, LW), F32),
            pltpu.VMEM((NB, KVL, LW, HD), F32),
            pltpu.VMEM((NB * BATCH, RB, HD), F32),
            dma((5,)),
            dma((1,)),
            dma((G,)),
            dma((1,)),
            dma((1,)),
            dma((T,)),
            dma((G,)),
            dma((NB,)),
            dma((NB,)),
            dma((NB,)),
            dma((NB,)),
            dma((1,)),
            dma((NB - 1,)),
            dma((1,)),
            dma((NB - 1,)),
        ],
        compiler_params=pltpu.CompilerParams(collective_id=0, has_side_effects=True),
    )(
        kept_tokens[None],
        prefill_slot[None],
        decode_slot[None],
        resident_kept,
        queries, new_entries, resident_cache, prefill_cache)


def solution(mesh):
    in_specs = (
        P("group", None, "tensor"),
        P("group", None, None),
        P("group", "tensor", None),
        P("group", "tensor", None),
        P(),
        P(),
        P(),
        P(),
    )
    out_specs = P("group", None, "tensor")
    return jax.shard_map(body, mesh=mesh, in_specs=in_specs, out_specs=out_specs, check_vma=False)
```

```python
import functools
import math

import jax
import jax.numpy as jnp
from jax import lax
from jax.experimental import pallas as pl
from jax.experimental.pallas import tpu as pltpu
from jax.sharding import PartitionSpec as P

H = 64
KVH = 8
HD = 128
STEPS = 4
MIG_DEV = 8
RES_DEV = 4
PER_GROUP = RES_DEV + MIG_DEV
BATCH = 4

NEG_FLOOR = -1e30
SCALE = 1.0 / math.sqrt(HD)
MESH = pl.DeviceIdType.MESH
F32 = jnp.float32
BF16 = jnp.bfloat16
NT = (((1,), (1,)), ((), ()))
TN = (((0,), (0,)), ((), ()))


def fill_table(G, g, kept_v, home_v, dest_v, tab_v):
    shape = (2 * G, dest_v.shape[1])
    n = lax.broadcasted_iota(jnp.int32, shape, 0)
    dest = jnp.broadcast_to(dest_v[...], shape)
    home = jnp.broadcast_to(home_v[...], shape)
    kept = jnp.broadcast_to(kept_v[...], shape)
    dest_group, home_group = lax.div(dest, PER_GROUP), lax.div(home, MIG_DEV)
    arriving = (dest_group == g) & (home_group == n)
    leaving = (home_group == g) & (dest_group == n - G)
    picked = jnp.where(arriving, dest - dest_group * PER_GROUP, 0)
    held = home - home_group * MIG_DEV + MIG_DEV * kept
    picked = picked + jnp.where(leaving, held, 0)
    total = jnp.sum(picked, axis=1, keepdims=True)
    tab_v[...] = jnp.broadcast_to(total, tab_v.shape)


def kernel(
    G,
    T,
    kept_v,
    home_v,
    dest_v,
    kept,
    q_hbm,
    new_hbm,
    res_hbm,
    pre_hbm,
    out,
    tab_v,
    tab_s,
    q_in,
    new_in,
    res,
    pre,
    qall,
    zq,
    stage,
    obuf,
    rbuf,
    sbuf,
    rstat,
    statbuf,
    facbuf,
    zo,
    zro,
    zs,
    zrs,
    newk,
    nstat,
    nadd,
    fin,
    cache_sem,
    zq_s,
    zq_r,
    rq_s,
    rq_r,
    f_s,
    f_r,
    o_s,
    o_r,
    st_s,
    st_r,
    zo_s,
    zo_r,
    zs_s,
    zs_r,
):
    KVL = max(1, KVH // T)
    HB = H // T
    HU = HB // KVL
    R = STEPS * HU
    LW = BATCH * R
    SW = 2 * KVL
    NB = 1 + G // BATCH
    pos = res.shape[1]
    half = KVH * HD
    g = lax.axis_index("group")
    t = lax.axis_index("tensor")
    offset = t * pos

    def peer_t(k):
        return lax.rem(t + k, T)

    def peer_g(k):
        return lax.rem(g + k, G)

    def from_g(k):
        return lax.rem(g - k + G, G)

    def over_t(src, dst, ssem, rsem, dev):
        return pltpu.make_async_remote_copy(
            src_ref=src, dst_ref=dst, send_sem=ssem, recv_sem=rsem,
            device_id=(g, dev), device_id_type=MESH,
        )

    def over_g(src, dst, ssem, rsem, dev):
        return pltpu.make_async_remote_copy(
            src_ref=src, dst_ref=dst, send_sem=ssem, recv_sem=rsem,
            device_id=(dev, t), device_id_type=MESH,
        )

    def c_zq(k):
        return over_g(zq.at[k], qall.at[t, RES_DEV + k], zq_s.at[0], zq_r.at[k], peer_g(k))

    def c_rq(k):
        p = peer_t(k)
        own = qall.at[t, pl.ds(0, RES_DEV)]
        return over_t(own, own, rq_s.at[0], rq_r.at[0], p)

    def c_fwd(k, n):
        own = qall.at[t, RES_DEV + k]
        return over_t(own, own, f_s.at[n], f_r.at[k], peer_t(n))

    def c_o(b, j, n):
        p = peer_t(n)
        rows = pl.ds(pl.multiple_of(j * R, R), R)
        return over_t(
            obuf.at[b, p, :, rows], rbuf.at[b, n, :, rows], o_s.at[b], o_r.at[b], p
        )

    def c_st(b, n):
        p = peer_t(n)
        return over_t(sbuf.at[b, p], rstat.at[b, n], st_s.at[b], st_r.at[b], p)

    def c_zo(k):
        return over_g(zo.at[k], zro.at[k], zo_s.at[0], zo_r.at[k // BATCH], from_g(k))

    def c_zs(k):
        return over_g(zs.at[k // BATCH], zrs.at[k], zs_s.at[0], zs_r.at[k // BATCH], from_g(k))

    barrier = pltpu.get_barrier_semaphore()
    for k in range(G - 1, 0, -1):
        pl.semaphore_signal(barrier, inc=1, device_id=(peer_g(k), t), device_id_type=MESH)
    for k in range(1, T):
        pl.semaphore_signal(barrier, inc=1, device_id=(g, peer_t(k)), device_id_type=MESH)
    load_q = pltpu.make_async_copy(q_hbm, q_in, cache_sem.at[2])
    load_new = pltpu.make_async_copy(new_hbm, new_in, cache_sem.at[3])
    load_res = pltpu.make_async_copy(res_hbm, res, cache_sem.at[0])
    load_pre = pltpu.make_async_copy(pre_hbm, pre, cache_sem.at[1])
    load_q.start()
    load_new.start()
    load_pre.start()
    load_res.start()
    fill_table(G, g, kept_v, home_v, dest_v, tab_v)
    load_tab = pltpu.make_async_copy(tab_v, tab_s, cache_sem.at[4])
    load_tab.start()
    load_tab.wait()
    load_q.wait()

    def arranged(row, slot):
        for h in range(HB):
            piece = q_in[row, :, h * HD : (h + 1) * HD]
            stage[slot, h * STEPS : (h + 1) * STEPS, :] = piece.astype(F32)
        return stage[slot].astype(BF16)

    for k in range(G):
        block = arranged(tab_s[peer_g(k), 0], k)
        zq[k] = block
        if k == 0:
            qall[t, RES_DEV] = block
    for j in range(RES_DEV):
        qall[t, j] = arranged(j, G + j)

    pl.semaphore_wait(barrier, G - 1 + T - 1)
    for k in range(1, G):
        c_zq(k).start()
    for n in range(1, T):
        c_rq(n).start()
    for n in range(1, T):
        c_fwd(0, n).start()

    load_new.wait()
    kv_col = pl.multiple_of((t * KVL * KVH) // (T * KVL) * HD, HD)
    for b in range(NB):
        for j in range(BATCH):
            row = j if b == 0 else tab_s[peer_g((b - 1) * BATCH + j), 0]
            lo = j * STEPS
            newk[b, 0, lo : lo + STEPS, :] = new_in[row, :, pl.ds(kv_col, KVL * HD)].astype(F32)
            newk[b, 1, lo : lo + STEPS, :] = new_in[
                row, :, pl.ds(pl.multiple_of(half + kv_col, HD), KVL * HD)
            ].astype(F32)

    def queries_of(b):
        return [
            jnp.concatenate(
                [
                    (qall[t, j] if b == 0 else zq[(b - 1) * BATCH + j])[i * R : (i + 1) * R]
                    for j in range(BATCH)
                ],
                axis=0,
            )
            for i in range(KVL)
        ]

    r16 = lax.broadcasted_iota(jnp.int32, (BATCH * STEPS, LW), 0)
    lanes16 = lax.broadcasted_iota(jnp.int32, (BATCH * STEPS, LW), 1)
    causal = (r16 // STEPS == lanes16 // R) & (r16 % STEPS <= lanes16 % STEPS)
    for b in range(NB):
        asked_b = queries_of(b)
        for i in range(KVL):
            keys = newk[b, 0, :, i * HD : (i + 1) * HD].astype(BF16)
            values = newk[b, 1, :, i * HD : (i + 1) * HD].astype(BF16)
            scores = lax.dot_general(keys, asked_b[i], NT, preferred_element_type=F32) * SCALE
            scores = jnp.where(causal, scores, NEG_FLOOR)
            top = jnp.max(scores, axis=0, keepdims=True)
            weights = jnp.where(causal, jnp.exp(scores - top), 0.0)
            nstat[b, i : i + 1, :] = top
            nstat[b, KVL + i : KVL + i + 1, :] = jnp.sum(weights, axis=0, keepdims=True)
            nadd[b, i] = lax.dot_general(
                weights.astype(BF16), values, TN, preferred_element_type=F32
            )

    for k in range(1, G):
        c_zq(k).wait_recv()
        for n in range(1, T):
            c_fwd(k, n).start()

    def attend_slot(cache, row, length, slot, b, j):
        lane = lax.broadcasted_iota(jnp.int32, (R, 128), 1)
        usable = offset + lax.broadcasted_iota(jnp.int32, (R, pos), 1) < length
        stat = jnp.zeros((R, 128), F32)
        rows = pl.ds(pl.multiple_of(j * R, R), R)
        W = 2 if KVL % 2 == 0 else 1
        units = [(tt, i) for tt in range(T) for i in range(0, KVL, W)]
        all_scores = []
        for tt, i in units:
            kv = (tt * KVL + i) * KVH // (T * KVL)
            asked = qall[tt, slot, i * R : (i + W) * R, :]
            keys = jnp.concatenate(
                [cache[row, :, (kv + w) * HD : (kv + w + 1) * HD] for w in range(W)], axis=0
            )
            scores = lax.dot_general(asked, keys, NT, preferred_element_type=F32)
            all_scores.append(
                [scores[w * R : (w + 1) * R, w * pos : (w + 1) * pos] * SCALE for w in range(W)]
            )
        all_weights = []
        for (tt, i), scores in zip(units, all_scores):
            rounded = []
            for w in range(W):
                masked = jnp.where(usable, scores[w], NEG_FLOOR)
                highest = jnp.max(masked, axis=1, keepdims=True)
                weights = jnp.where(usable, jnp.exp(masked - highest), 0.0)
                total = jnp.sum(weights, axis=1, keepdims=True)
                rounded.append(weights.astype(BF16))
                stat = jnp.where(lane == tt * SW + i + w, highest, stat)
                stat = jnp.where(lane == tt * SW + KVL + i + w, total, stat)
            all_weights.append(jnp.concatenate(rounded, axis=0))
        for (tt, i), weights in zip(units, all_weights):
            kv = (tt * KVL + i) * KVH // (T * KVL)
            values = cache[row, :, half + kv * HD : half + (kv + W) * HD]
            blended = jnp.dot(weights, values, preferred_element_type=F32)
            for w in range(W):
                obuf[b, tt, i + w, rows, :] = blended[
                    w * R : (w + 1) * R, w * HD : (w + 1) * HD
                ].astype(BF16)
        statbuf[rows, :] = stat
        for n in range(1, T):
            c_o(b, j, n).start()

    def send_batch(b):
        turned = statbuf[...].T
        for tt in range(T):
            sbuf[b, tt] = turned[tt * SW : tt * SW + 8, :]
        for n in range(1, T):
            c_st(b, n).start()
        rbuf[b, 0] = obuf[b, t]
        rstat[b, 0] = sbuf[b, t]

    rest = pl.ds(1, T - 1)
    load_pre.wait()

    @pl.loop(1, NB)
    def _(b):
        @pl.loop(0, BATCH)
        def _(j):
            k = (b - 1) * BATCH + j
            spread = qall.at[rest, RES_DEV + k]
            over_t(spread, spread, f_s.at[0], f_r.at[k], t).wait_recv()
            source = from_g(k)
            held = tab_s[G + source, 0]
            attend_slot(pre, held % MIG_DEV, held // MIG_DEV, RES_DEV + k, b, j)

        send_batch(b)

    load_res.wait()
    q_rest = qall.at[rest, pl.ds(0, RES_DEV)]
    over_t(q_rest, q_rest, rq_s.at[0], rq_r.at[0], t).wait_recv()

    @pl.loop(0, RES_DEV)
    def _(j):
        attend_slot(res, j, kept[g * RES_DEV + j], j, 0, j)

    send_batch(0)
    def merged(b):
        over_t(rstat.at[b, rest], rstat.at[b, rest], st_s.at[b], st_r.at[b], t).wait_recv()
        over_t(rbuf.at[b, rest], rbuf.at[b, rest], o_s.at[b], o_r.at[b], t).wait_recv()
        tops = [rstat[b, n][:KVL] for n in range(T)]
        highest = functools.reduce(jnp.maximum, tops)
        total = jnp.zeros((KVL, LW), F32)
        for n in range(T):
            factor = jnp.exp(tops[n] - highest)
            total = total + factor * rstat[b, n][KVL:SW]
            facbuf[n * KVL : (n + 1) * KVL, :] = factor
        columns = facbuf[...].T
        blended = []
        for i in range(KVL):
            sum_i = jnp.zeros((LW, HD), F32)
            for n in range(T):
                c = n * KVL + i
                sum_i = sum_i + rbuf[b, n, i].astype(F32) * columns[:, c : c + 1]
            blended.append(sum_i)
        return highest, total, blended

    def finish(b, highest, total, blended):
        new_top, new_total = nstat[b, 0:KVL], nstat[b, KVL:SW]
        top = jnp.maximum(highest, new_top)
        old_part, new_part = jnp.exp(highest - top), jnp.exp(new_top - top)
        inverse = 1.0 / (total * old_part + new_total * new_part)
        facbuf[0:KVL, :] = old_part * inverse
        facbuf[KVL:SW, :] = new_part * inverse
        columns = facbuf[...].T
        for i in range(KVL):
            done = blended[i] * columns[:, i : i + 1]
            done = done + nadd[b, i] * columns[:, KVL + i : KVL + i + 1]
            for j in range(BATCH):
                fin[b * BATCH + j, i * R : (i + 1) * R, :] = done[j * R : (j + 1) * R]

    def put(slot, row):
        for h in range(HB):
            piece = fin[slot, h * STEPS : (h + 1) * STEPS, :]
            out[row, :, h * HD : (h + 1) * HD] = piece.astype(BF16)

    for b in range(1, NB):
        highest, total, blended = merged(b)
        packed = jnp.concatenate([highest, total], axis=0)
        zs[b - 1, 0:SW, :] = packed
        for j in range(BATCH):
            k = (b - 1) * BATCH + j
            for i in range(KVL):
                zo[k, i] = blended[i][j * R : (j + 1) * R].astype(BF16)
            if k:
                c_zs(k).start()
                c_zo(k).start()
            else:
                zrs[0] = zs[0]
                zro[0] = zo[0]

    finish(0, *merged(0))
    for j in range(RES_DEV):
        put(j, j)

    for b in range(1, NB):
        lanes = lax.broadcasted_iota(jnp.int32, (8, LW), 1)
        stats = jnp.zeros((8, LW), F32)
        first = (b - 1) * BATCH
        came = pl.ds(max(first, 1), first + BATCH - max(first, 1))
        over_g(zrs.at[came], zrs.at[came], zs_s.at[0], zs_r.at[b - 1], g).wait_recv()
        over_g(zro.at[came], zro.at[came], zo_s.at[0], zo_r.at[b - 1], g).wait_recv()
        for j in range(BATCH):
            k = (b - 1) * BATCH + j
            stats = jnp.where(lanes // R == j, zrs[k], stats)
        blended = [
            jnp.concatenate(
                [zro[(b - 1) * BATCH + j, i].astype(F32) for j in range(BATCH)], axis=0
            )
            for i in range(KVL)
        ]
        finish(b, stats[:KVL], stats[KVL:SW], blended)
    for l in range(MIG_DEV):
        k_of = 0
        for k in range(1, G):
            k_of = jnp.where(tab_s[peer_g(k), 0] == RES_DEV + l, k, k_of)
        put(RES_DEV + k_of, RES_DEV + l)

    others = pl.ds(1, G - 1)
    over_g(zq.at[others], zq.at[others], zq_s.at[0], zq_r.at[0], g).wait_send()
    over_g(zrs.at[others], zrs.at[others], zs_s.at[0], zs_r.at[0], g).wait_send()
    over_g(zo.at[others], zo.at[others], zo_s.at[0], zo_r.at[0], g).wait_send()
    over_t(q_rest, q_rest, rq_s.at[0], rq_r.at[0], t).wait_send()
    passed = qall.at[0, pl.ds(RES_DEV, G)]
    for n in range(1, T):
        over_t(passed, passed, f_s.at[n], f_r.at[0], t).wait_send()
    for b in range(NB):
        over_t(rstat.at[b, rest], rstat.at[b, rest], st_s.at[b], st_r.at[b], t).wait_send()
        over_t(rbuf.at[b, rest], rbuf.at[b, rest], o_s.at[b], o_r.at[b], t).wait_send()


def body(
    queries,
    new_entries,
    resident_cache,
    prefill_cache,
    resident_kept,
    kept_tokens,
    prefill_slot,
    decode_slot,
):
    G = lax.axis_size("group")
    T = lax.axis_size("tensor")
    KVL = max(1, KVH // T)
    HB = H // T
    RB = STEPS * HB
    R = RB // KVL
    LW = BATCH * R
    NB = 1 + G // BATCH
    dma = pltpu.SemaphoreType.DMA
    vmem = pl.BlockSpec(memory_space=pltpu.VMEM)
    smem = pl.BlockSpec(memory_space=pltpu.SMEM)
    hbm = pl.BlockSpec(memory_space=pl.ANY)
    return pl.pallas_call(
        functools.partial(kernel, G, T),
        out_shape=pltpu.VMEM(queries.shape, BF16),
        in_specs=[vmem, vmem, vmem, smem, hbm, hbm, hbm, hbm],
        out_specs=vmem,
        scratch_shapes=[
            pltpu.VMEM((2 * G, 128), jnp.int32),
            pltpu.SMEM((2 * G, 128), jnp.int32),
            pltpu.VMEM(queries.shape, BF16),
            pltpu.VMEM(new_entries.shape, BF16),
            pltpu.VMEM(resident_cache.shape, BF16),
            pltpu.VMEM(prefill_cache.shape, BF16),
            pltpu.VMEM((T, RES_DEV + G, RB, HD), BF16),
            pltpu.VMEM((G, RB, HD), BF16),
            pltpu.VMEM((G + RES_DEV, RB, HD), F32),
            pltpu.VMEM((NB, T, KVL, LW, HD), BF16),
            pltpu.VMEM((NB, T, KVL, LW, HD), BF16),
            pltpu.VMEM((NB, T, 8, LW), F32),
            pltpu.VMEM((NB, T, 8, LW), F32),
            pltpu.VMEM((LW, 128), F32),
            pltpu.VMEM((128, LW), F32),
            pltpu.VMEM((G, KVL, R, HD), BF16),
            pltpu.VMEM((G, KVL, R, HD), BF16),
            pltpu.VMEM((NB - 1, 8, LW), F32),
            pltpu.VMEM((G, 8, LW), F32),
            pltpu.VMEM((NB, 2, BATCH * STEPS, KVL * HD), F32),
            pltpu.VMEM((NB, 8, LW), F32),
            pltpu.VMEM((NB, KVL, LW, HD), F32),
            pltpu.VMEM((NB * BATCH, RB, HD), F32),
            dma((5,)),
            dma((1,)),
            dma((G,)),
            dma((1,)),
            dma((1,)),
            dma((T,)),
            dma((G,)),
            dma((NB,)),
            dma((NB,)),
            dma((NB,)),
            dma((NB,)),
            dma((1,)),
            dma((NB - 1,)),
            dma((1,)),
            dma((NB - 1,)),
        ],
        compiler_params=pltpu.CompilerParams(collective_id=0, has_side_effects=True),
    )(
        kept_tokens[None],
        prefill_slot[None],
        decode_slot[None],
        resident_kept,
        queries, new_entries, resident_cache, prefill_cache)


def solution(mesh):
    in_specs = (
        P("group", None, "tensor"),
        P("group", None, None),
        P("group", "tensor", None),
        P("group", "tensor", None),
        P(),
        P(),
        P(),
        P(),
    )
    out_specs = P("group", None, "tensor")
    return jax.shard_map(body, mesh=mesh, in_specs=in_specs, out_specs=out_specs, check_vma=False)
```
